32 devices in a mesh: fsdp: 2 (over x), ctx: 2 (over core), tp: 8 (over z, y).
Axes of the slice: x: 2, y: 2, z: 4, core: 2. Of those that a mesh axis runs over, the one named last changes fastest.
Arguments:
- inputs: bfloat16 [8, 1024, 1024], P('fsdp', ('ctx', 'tp')), may hold values from -6 to 6
- timesteps: int32 [8], replicated, may hold values from 0 to 4999
- segments: int32 [8, 1024], P('fsdp'), may hold values from 0 to 11, never falling along the last dimension, each value on 1 to 512 neighbouring positions
- table: bfloat16 [5000, 1024], replicated, may hold values from -3 to 3
- w_qkv: bfloat16 [3, 1024, 1024], P(None, 'fsdp', 'tp'), may hold values from -0.1875 to 0.1875
- qv_bias: bfloat16 [2, 1024], P(None, 'tp'), may hold values from -3 to 3
- w_out: bfloat16 [1024, 1024], P('tp', 'fsdp'), may hold values from -0.75 to 0.75
- w_up: bfloat16 [1024, 4096], P('fsdp', 'tp'), may hold values from -0.1875 to 0.1875
- ffn_bias: bfloat16 [4096], P('tp'), may hold values from -3 to 3
- w_down: bfloat16 [4096, 1024], P('tp', 'fsdp'), may hold values from -0.09375 to 0.09375
- out_biases: bfloat16 [2, 1024], replicated, may hold values from -2 to 2
- norm_gains: bfloat16 [2, 1024], replicated, may hold values from 0.5 to 1.5
- norm_biases: bfloat16 [2, 1024], replicated, may hold values from -2 to 2
- cotangent: bfloat16 [8, 1024, 1024], P('fsdp', ('ctx', 'tp')), may hold values from -6 to 6
Outputs:
- output: bfloat16 [8, 1024, 1024], P('fsdp', ('ctx', 'tp'))
- grad_inputs: bfloat16 [8, 1024, 1024], P('fsdp', ('ctx', 'tp'))
- grad_table: float32 [5000, 1024], P(None, 'fsdp')
- grad_qkv: float32 [3, 1024, 1024], P(None, ('fsdp', 'ctx'), 'tp')
- grad_qv_bias: float32 [2, 1024], replicated
- grad_out: float32 [1024, 1024], P('tp', ('fsdp', 'ctx'))
- up_weight_gradient: float32 [1024, 4096], P(('fsdp', 'ctx'), 'tp')
- grad_ffn_bias: float32 [4096], replicated
- grad_down: float32 [4096, 1024], P('tp', ('fsdp', 'ctx'))
- grad_out_biases: float32 [2, 1024], replicated
- grad_norm_gains: float32 [2, 1024], replicated
- grad_norm_biases: float32 [2, 1024], replicated
The draws below stay inside these ranges and needn't reach their ends.
Inputs may be any that keep to these rules, and one draw needn't show every extreme that they name: `segments`: in each sequence the segment numbers never fall; each document holds 1 to 1024 // 2 tokens and some document holds exactly that many.
All inputs are finite; a program needn't handle non-finite values.
Results may differ from the reference program's by a relative error of at most 0.02.
Values may be sent and summed in bfloat16 or wider, within the bound.
No kernel may reach another device: no remote copies, remote signals or barrier semaphores. Data moves between devices by JAX's collectives and lax.ppermute only.
A program may use at most 128 MiB of HBM per device.

```python
import math
import jax
import jax.numpy as jnp
import numpy as np
from jax import lax

D = 1024
HEADS = 16
HEAD = 64
FF = 4096
NSTEPS = 5000
LEN = 1024
DOCS = 12
SEQS = 8


def place_ends(values, stream_key, smallest, top_value):
    longest = values.shape.index(max(values.shape))
    spots = []
    for shift in (0, 1):
        where = [jax.random.randint(jax.random.fold_in(stream_key, axis), (), 0, length) for axis, length in enumerate(values.shape)]
        where[longest] = (where[longest] + shift) % values.shape[longest]
        spots.append(tuple(where))
    return values.at[spots[0]].set(smallest).at[spots[1]].set(top_value)


def shard_levels(key, shape, cuts, low, top_value):
    def one(position, shards_of):
        draws = jax.random.uniform(jax.random.fold_in(jax.random.fold_in(key, 6), position), (shards_of,), jnp.float32, low / len(cuts), top_value / len(cuts))
        return jnp.repeat(jnp.exp(draws), shape[position] // shards_of).reshape((-1,) + (1,) * (len(shape) - position - 1))

    factor_of = one(*cuts[0])
    for cut in cuts[1:]:
        factor_of = factor_of * one(*cut)
    return factor_of


def split_up(amount, total, most, slope):
    portions = [(1 << 20) // math.isqrt(grade ** slope) + 1 for grade in range(2, amount + 1)]
    surplus, given = total - most - (amount - 1), [1] * (amount - 1)
    while surplus > 0:
        candidates = [i for i in range(amount - 1) if given[i] < most]
        whole, left = sum([portions[i] for i in candidates]), surplus
        for i in candidates:
            addition = min(most - given[i], max(1, left * portions[i] // whole), surplus)
            given[i] = given[i] + addition
            surplus = surplus - addition
    return np.array([most] + given)


def ragged(rng, amount, total, bound, slope):
    if amount == 2:
        one = jax.random.randint(rng, (), max(1, total - bound), min(bound, total - 1) + 1)
        return jnp.stack([one, total - one])
    tallies = jnp.asarray(split_up(amount, total, bound, slope), jnp.int32)
    couples = (amount - 1) // 2
    giver, receiver = tallies[1:1 + 2 * couples:2], tallies[2:2 + 2 * couples:2]
    room = jnp.minimum(giver - 1, bound - receiver)
    moved = jax.random.randint(jax.random.fold_in(rng, 1), (couples,), 0, 1 << 20) % (room + 1)
    tallies = tallies.at[1:1 + 2 * couples:2].set(giver - moved).at[2:2 + 2 * couples:2].set(receiver + moved)
    return tallies[jax.random.permutation(jax.random.fold_in(rng, 2), amount)]


def scatter_about(stream_key, shape, scale, bound, split=(), held_as=jnp.bfloat16):
    loudness = shard_levels(stream_key, shape, split, -0.22, 0.18) if split else 1.0
    values = jax.random.normal(stream_key, shape, jnp.float32) * scale * loudness
    return jnp.minimum(jnp.maximum(values, -bound), bound).astype(held_as)


def setup_inputs(seed: int = 0) -> dict:
    streams_of = jax.random.split(jax.random.key(seed), 15)
    inputs = scatter_about(streams_of[0], (SEQS, LEN, D), 1.0, 6.0, ((0, 2), (1, 16)))
    timesteps = place_ends(jax.random.randint(streams_of[1], (SEQS,), 0, NSTEPS), jax.random.fold_in(streams_of[1], 1), 0, NSTEPS - 1).astype(jnp.int32)
    segments = jax.vmap(lambda own: jnp.searchsorted(jnp.cumsum(ragged(own, DOCS, LEN, LEN // 2, 2)), jnp.arange(LEN), side="right"))(jax.random.split(streams_of[2], SEQS)).reshape((SEQS, LEN)).astype(jnp.int32)
    table = scatter_about(streams_of[3], (NSTEPS, D), 0.5, 3.0)
    w_qkv = scatter_about(streams_of[4], (3, D, D), D ** -0.5, 0.1875, ((1, 2), (2, 8)))
    qv_bias = scatter_about(streams_of[5], (2, D), 0.5, 3.0, ((1, 8),))
    w_out = scatter_about(streams_of[6], (D, D), HEAD ** -0.5, 0.75, ((0, 8), (1, 2)))
    w_up = scatter_about(streams_of[7], (D, FF), D ** -0.5, 0.1875, ((0, 2), (1, 8)))
    ffn_bias = scatter_about(streams_of[8], (FF,), 0.5, 3.0, ((0, 8),))
    w_down = scatter_about(streams_of[9], (FF, D), FF ** -0.5, 0.09375, ((0, 8), (1, 2)))
    out_biases = scatter_about(streams_of[10], (2, D), 0.3, 2.0)
    norm_gains = jnp.clip(1.0 + 0.1 * jax.random.normal(streams_of[11], (2, D), jnp.float32), 0.5, 1.5).astype(jnp.bfloat16)
    norm_biases = scatter_about(streams_of[12], (2, D), 0.3, 2.0)
    cotangent = scatter_about(streams_of[13], (SEQS, LEN, D), 1.0, 6.0, ((0, 2), (1, 16)))
    return dict(inputs=inputs, timesteps=timesteps, segments=segments, table=table, w_qkv=w_qkv, qv_bias=qv_bias, w_out=w_out, w_up=w_up, ffn_bias=ffn_bias, w_down=w_down, out_biases=out_biases, norm_gains=norm_gains, norm_biases=norm_biases, cotangent=cotangent)


@jax.custom_vjp
def low(v):
    return lax.optimization_barrier(v.astype(jnp.bfloat16)).astype(jnp.float32)

@jax.custom_vjp
def low_back(v):
    return v

def low_keep(v):
    return (low(v), None)

def low_pass(kept, grad):
    return (grad,)

def back_keep(v):
    return (v, None)

def back_low(kept, grad):
    return (low(grad),)
low.defvjp(low_keep, low_pass)
low_back.defvjp(back_keep, back_low)
HIGHEST = lax.Precision.HIGHEST
NORM_EPS = 1e-05
MASKED = -1e+30

def layer_norm(residual, gain, offset):
    row_mean = lax.optimization_barrier(jnp.mean(residual, axis=-1, keepdims=True))
    centered = residual - row_mean
    variance = lax.optimization_barrier(jnp.mean(centered * centered, axis=-1, keepdims=True))
    return centered * lax.rsqrt(variance + NORM_EPS) * gain + offset

def attend_sequence(operands):
    query, key_rows, value_rows, documents = operands
    raw_scores = low_back(jnp.einsum('qhd,khd->hqk', query, key_rows, precision=HIGHEST) * HEAD ** (-0.5))
    same_doc = documents[:, None] == documents[None, :]
    masked_scores = jnp.where(same_doc[None], raw_scores, MASKED)
    weights = low(jax.nn.softmax(masked_scores, axis=-1))
    return jnp.einsum('hqk,khd->qhd', weights, value_rows, precision=HIGHEST)

def block_forward(inputs, table, w_qkv, qv_bias, w_out, w_up, ffn_bias, w_down, out_biases, norm_gains, norm_biases, step_group, doc_group):
    group = inputs.shape[0]
    start = inputs + jnp.take(table, step_group, axis=0)[:, None, :]
    lowered = low(start)
    projected_rows = jnp.einsum('gld,cde->cgle', lowered, w_qkv, precision=HIGHEST)
    head_shape = (group, LEN, HEADS, HEAD)
    query = low(low_back(projected_rows[0] + qv_bias[0])).reshape(head_shape)
    key_rows = low(low_back(projected_rows[1])).reshape(head_shape)
    value_rows = low(low_back(projected_rows[2] + qv_bias[1])).reshape(head_shape)
    mixed = lax.map(jax.checkpoint(attend_sequence), (query, key_rows, value_rows, doc_group))
    mixed = low(low_back(mixed.reshape(group, LEN, D)))
    attended = low_back(jnp.einsum('gle,ed->gld', mixed, w_out, precision=HIGHEST) + out_biases[0])
    hidden = layer_norm(start + attended, norm_gains[0], norm_biases[0])
    pre_act = low_back(jnp.einsum('gld,df->glf', low(hidden), w_up, precision=HIGHEST) + ffn_bias)
    gelu_activation = low(jax.nn.gelu(pre_act, approximate=False))
    ffn_out = low_back(jnp.einsum('glf,fd->gld', gelu_activation, w_down, precision=HIGHEST) + out_biases[1])
    return layer_norm(hidden + ffn_out, norm_gains[1], norm_biases[1])

def reference(inputs, timesteps, segments, table, w_qkv, qv_bias, w_out, w_up, ffn_bias, w_down, out_biases, norm_gains, norm_biases, cotangent):
    params = tuple((weight.astype(jnp.float32) for weight in (table, w_qkv, qv_bias, w_out, w_up, ffn_bias, w_down, out_biases, norm_gains, norm_biases)))
    group = math.gcd(SEQS, max(1, 4096 // LEN))
    blocks = SEQS // group
    x_groups = inputs.astype(jnp.float32).reshape(blocks, group, LEN, D)
    ct_groups = cotangent.astype(jnp.float32).reshape(blocks, group, LEN, D)
    step_groups = timesteps.reshape(blocks, group)
    doc_groups = segments.reshape(blocks, group, LEN)

    def accumulate(carry, element):
        x_group, ct_group, step_group, doc_group = element

        def forward(x_in, *weights):
            return block_forward(x_in, *weights, step_group, doc_group)
        result, pull = jax.vjp(forward, x_group, *params)
        grads = pull(ct_group)
        carry = tuple((summed + fresh for summed, fresh in zip(carry, grads[1:])))
        return (carry, (result, grads[0]))
    zeros = tuple((jnp.zeros(weight.shape, jnp.float32) for weight in params))
    totals, (results, grad_groups) = lax.scan(accumulate, zeros, (x_groups, ct_groups, step_groups, doc_groups))
    output = results.reshape(SEQS, LEN, D).astype(jnp.bfloat16)
    grad_inputs = grad_groups.reshape(SEQS, LEN, D).astype(jnp.bfloat16)
    return (output, grad_inputs, totals[0], totals[1], totals[2], totals[3], totals[4], totals[5], totals[6], totals[7], totals[8], totals[9])
```

```python
import jax
import jax.numpy as jnp
from jax import lax
from jax.sharding import Mesh
from jax.sharding import PartitionSpec as P

HEAD = 64
NORM_EPS = 1e-05
MASKED = -1e30
F32 = jnp.float32
BF16 = jnp.bfloat16


def swap(rows, axis):
    return lax.ppermute(rows, axis, [(0, 1), (1, 0)])


def pick(parts, index, at):
    return lax.dynamic_index_in_dim(parts, index, at, keepdims=False)


def gather_new(rows, axis, at):
    if lax.axis_size(axis) != 2:
        return lax.all_gather(rows, axis, axis=at, tiled=False)
    shape = [1] * (rows.ndim + 1)
    shape[at] = 2
    own = (jnp.arange(2) == lax.axis_index(axis)).reshape(shape)
    return jnp.where(own, jnp.expand_dims(rows, at), jnp.expand_dims(swap(rows, axis), at))


def scatter_new(parts, axis, at):
    if lax.axis_size(axis) != 2:
        return lax.psum_scatter(
            parts.astype(BF16), axis, scatter_dimension=at, tiled=False
        ).astype(F32)
    here = lax.axis_index(axis)
    away = swap(pick(parts, 1 - here, at).astype(BF16), axis)
    return pick(parts, here, at).astype(F32) + away.astype(F32)


def exchange(pieces, axis):
    size = lax.axis_size(axis)
    here = lax.axis_index(axis)
    result = jnp.zeros_like(pieces)
    result = lax.dynamic_update_index_in_dim(result, pick(pieces, here, 0), here, 0)
    for step in range(1, size):
        sent = pick(pieces, (here + step) % size, 0)
        ring = [(one, (one + step) % size) for one in range(size)]
        got = lax.ppermute(sent, axis, ring)
        result = lax.dynamic_update_index_in_dim(result, got, (here - step) % size, 0)
    return result


def total(values, axes):
    for axis in axes:
        size = lax.axis_size(axis)
        if size & (size - 1):
            values = lax.psum(values, axis)
            continue
        step = 1
        while step < size:
            values = values + lax.ppermute(values, axis, [(one, one ^ step) for one in range(size)])
            step *= 2
    return values


def norm(rows):
    centered = rows - jnp.mean(rows, axis=-1, keepdims=True)
    inverse = lax.rsqrt(jnp.mean(centered * centered, axis=-1, keepdims=True) + NORM_EPS)
    return centered * inverse, inverse


def norm_back(normed, inverse, gain, grad):
    scaled = grad * gain
    mean_one = jnp.mean(scaled, axis=-1, keepdims=True)
    mean_two = jnp.mean(scaled * normed, axis=-1, keepdims=True)
    return (scaled - mean_one - normed * mean_two) * inverse


def dot(left, right, dims):
    return lax.dot_general(left, right, (dims, ((), ())), preferred_element_type=F32)


NN = ((1,), (0,))
NT = ((1,), (1,))
TN = ((0,), (0,))


def contract(rows, weight):
    width = weight.shape[2]
    result = None
    for part in range(weight.shape[0]):
        term = dot(rows[:, part * width : (part + 1) * width], weight[part], NT)
        result = term if result is None else result + term
    return result


def expand(rows, weight):
    return jnp.concatenate(
        [dot(rows, weight[part], NN).astype(BF16) for part in range(weight.shape[0])], axis=1
    )


def outer(left, right, fsdp_size):
    width = right.shape[1] // fsdp_size
    return jnp.stack(
        [
            dot(left, right[:, part * width : (part + 1) * width], TN).astype(BF16)
            for part in range(fsdp_size)
        ]
    )


def shards(
    inputs,
    timesteps,
    segments,
    table,
    w_qkv,
    qv_bias,
    w_out,
    w_up,
    ffn_bias,
    w_down,
    out_biases,
    norm_gains,
    norm_biases,
    cotangent,
):
    fsdp_size, ctx_size = lax.axis_size("fsdp"), lax.axis_size("ctx")
    tz_size, ty_size = lax.axis_size("tz"), lax.axis_size("ty")
    fsdp_at, ctx_at = lax.axis_index("fsdp"), lax.axis_index("ctx")
    tz_at, ty_at = lax.axis_index("tz"), lax.axis_index("ty")
    everywhere = ("ctx", "ty", "fsdp", "tz")
    seq_here, piece, model = inputs.shape
    length = segments.shape[1]
    part = model // fsdp_size
    scale = HEAD ** (-0.5)
    columns = w_qkv.shape[2]
    block_heads = columns // HEAD
    heads = tz_size * block_heads // ctx_size
    early = block_heads % ctx_size == 0

    def collect(block, groups):
        rows = block.shape[0]
        if early:
            kept = pick(block.reshape(groups, ctx_size, rows // (groups * ctx_size), part), ctx_at, 1)
            kept = kept.reshape(rows // ctx_size, part)
            full = lax.all_gather(kept, ("fsdp", "tz"), axis=0, tiled=True)
            return full.reshape(fsdp_size, tz_size * rows // ctx_size, part)
        full = lax.all_gather(block, ("fsdp", "tz"), axis=0, tiled=True)
        full = full.reshape(fsdp_size, ctx_size, tz_size * rows // ctx_size, part)
        return pick(full, ctx_at, 1)

    qkv_block = jnp.transpose(w_qkv.reshape(3, part, block_heads, HEAD), (2, 0, 3, 1))
    qkv_all = collect(qkv_block.reshape(3 * columns, part), 1)
    out_all = collect(w_out, 1)
    up_all = collect(w_up.T, 1)
    down_all = collect(w_down, 1)

    def own_share(values):
        lead = values.shape[:-1]
        if early:
            kept = pick(values.reshape(lead + (ctx_size, -1)), ctx_at, values.ndim - 1)
            return lax.all_gather(kept, "tz", axis=values.ndim - 1, tiled=True)
        full = lax.all_gather(values, "tz", axis=values.ndim - 1, tiled=True)
        return pick(full.reshape(lead + (ctx_size, -1)), ctx_at, values.ndim - 1)

    qv_own = own_share(qv_bias).astype(F32)
    ffn_own = own_share(ffn_bias[None])[0].astype(F32)
    biases_out = out_biases.astype(F32)
    gains = norm_gains.astype(F32)
    offsets = norm_biases.astype(F32)

    sequence = fsdp_at * seq_here + tz_at
    docs = pick(segments, tz_at, 0)
    step_row = lax.dynamic_slice_in_dim(table, timesteps[sequence], 1, 0).astype(F32)
    own_inputs = exchange(inputs, "tz")
    own_rows = own_inputs.reshape(tz_size * piece, model)

    def row_gather(rows):
        grid = gather_new(rows.reshape(tz_size, piece, model), "ty", 1)
        return gather_new(grid, "ctx", 0).reshape(length, model)

    def row_sum(partial):
        grid = partial.reshape(ctx_size, tz_size, ty_size, piece, model)
        return scatter_new(scatter_new(grid, "ctx", 0), "ty", 1).reshape(tz_size * piece, model)

    start = own_rows.astype(F32) + step_row
    lowered = (row_gather(own_rows).astype(F32) + step_row).astype(BF16)

    projected = contract(lowered, qkv_all).reshape(length, heads, 3, HEAD)
    qv_heads = qv_own.reshape(2, heads, HEAD)
    query = (projected[:, :, 0] + qv_heads[0]).astype(BF16)
    key = projected[:, :, 1].astype(BF16)
    value = (projected[:, :, 2] + qv_heads[1]).astype(BF16)

    same_doc = docs[:, None] == docs[None, :]

    def scores_of(query, key):
        raw = jnp.einsum("qhd,khd->hqk", query, key, preferred_element_type=F32) * scale
        return jnp.where(same_doc[None], raw, MASKED)

    scores = scores_of(query, key)
    row_max = jnp.max(scores, axis=-1, keepdims=True)
    log_total = row_max + jnp.log(jnp.sum(jnp.exp(scores - row_max), axis=-1, keepdims=True))
    weights = jnp.exp(scores - log_total).astype(BF16)
    mixed = jnp.einsum("hqk,khd->qhd", weights, value, preferred_element_type=F32).astype(BF16)
    mixed = mixed.reshape(length, heads * HEAD)

    attended = row_sum(expand(mixed, out_all)) + biases_out[0]
    normed_one, inverse_one = norm(start + attended)
    hidden = normed_one * gains[0] + offsets[0]
    hidden_rows = row_gather(hidden.astype(BF16))
    pre_act = contract(hidden_rows, up_all) + ffn_own
    cdf = 0.5 * (1.0 + lax.erf(pre_act * (0.5**0.5)))
    activated = (pre_act * cdf).astype(BF16)
    slope = cdf + pre_act * jnp.exp(-0.5 * pre_act * pre_act) * (0.5 / jnp.pi) ** 0.5
    ffn_out = row_sum(expand(activated, down_all)) + biases_out[1]
    normed_two, inverse_two = norm(hidden + ffn_out)
    own_output = (normed_two * gains[1] + offsets[1]).astype(BF16)
    output = exchange(own_output.reshape(tz_size, piece, model), "tz")

    grad_final = exchange(cotangent, "tz").reshape(tz_size * piece, model).astype(F32)
    grad_second = norm_back(normed_two, inverse_two, gains[1], grad_final)
    grad_ffn = grad_second.astype(BF16)
    grad_ffn_rows = row_gather(grad_ffn)
    grad_pre = (contract(grad_ffn_rows, down_all) * slope).astype(BF16)
    grad_down = outer(activated, grad_ffn_rows, fsdp_size)
    grad_up = outer(grad_pre, hidden_rows, fsdp_size)
    grad_hidden = grad_second + row_sum(expand(grad_pre, up_all))
    grad_first = norm_back(normed_one, inverse_one, gains[0], grad_hidden)
    grad_attended = grad_first.astype(BF16)
    grad_attended_rows = row_gather(grad_attended)
    grad_out = outer(mixed, grad_attended_rows, fsdp_size)
    grad_mixed = contract(grad_attended_rows, out_all).astype(BF16).reshape(length, heads, HEAD)

    probabilities = jnp.exp(scores_of(query, key) - log_total)
    grad_weights = jnp.einsum("qhd,khd->hqk", grad_mixed, value, preferred_element_type=F32)
    row_dot = jnp.sum(probabilities * grad_weights, axis=-1, keepdims=True)
    grad_scores = (probabilities * (grad_weights - row_dot)).astype(BF16)
    grad_query = jnp.einsum("hqk,khd->qhd", grad_scores, key, preferred_element_type=F32) * scale
    grad_key = jnp.einsum("hqk,qhd->khd", grad_scores, query, preferred_element_type=F32) * scale
    grad_value = jnp.einsum(
        "hqk,qhd->khd", probabilities.astype(BF16), grad_mixed, preferred_element_type=F32
    )
    grad_heads = jnp.stack(
        [grad_query.astype(BF16), grad_key.astype(BF16), grad_value.astype(BF16)], axis=2
    ).reshape(length, heads * 3 * HEAD)
    grad_qkv = outer(grad_heads, lowered, fsdp_size)
    grad_start = grad_first + row_sum(expand(grad_heads, qkv_all))
    grad_inputs = exchange(grad_start.astype(BF16).reshape(tz_size, piece, model), "tz")

    def release(grads):
        rows = grads.shape[1]
        if early:
            own = lax.psum_scatter(
                grads.reshape(fsdp_size * rows, part),
                ("fsdp", "tz"),
                scatter_dimension=0,
                tiled=True,
            )
            share = rows // tz_size
            halves = own.reshape(share, ctx_size, part // ctx_size)
            if ctx_size == 2:
                own_half = pick(halves, ctx_at, 1)
                away = swap(pick(halves, 1 - ctx_at, 1), "ctx")
                order = (jnp.arange(2) == ctx_at)[:, None, None]
                both = jnp.where(order, own_half[None], away[None])
            else:
                both = lax.all_to_all(jnp.moveaxis(halves, 1, 0), "ctx", 0, 0, tiled=True)
            return both.reshape(ctx_size * share, part // ctx_size).astype(F32)
        full = jnp.zeros((fsdp_size, ctx_size, rows, part), BF16)
        full = lax.dynamic_update_index_in_dim(full, grads, ctx_at, 1)
        full = full.reshape(fsdp_size, tz_size, ctx_size * rows // tz_size, ctx_size, -1)
        full = jnp.transpose(full, (0, 3, 1, 2, 4))
        own = lax.psum_scatter(
            full.reshape((fsdp_size * ctx_size,) + full.shape[2:]),
            ("fsdp", "ctx"),
            scatter_dimension=0,
            tiled=False,
        )
        return lax.psum_scatter(own, "tz", scatter_dimension=0, tiled=False).astype(F32)

    red_down = release(grad_down)
    red_up = release(grad_up).T
    red_out = release(grad_out)
    red_qkv = jnp.transpose(
        release(grad_qkv).reshape(block_heads, 3, HEAD, part // ctx_size), (1, 3, 0, 2)
    ).reshape(3, part // ctx_size, columns)

    def spread(values):
        lead = values.shape[:-1]
        at = len(lead)
        block = values.shape[-1] * ctx_size // tz_size
        if early:
            full = jnp.zeros(lead + (tz_size, ty_size, ctx_size, block // ctx_size), F32)
            own = values.reshape(lead + (tz_size, 1, 1, block // ctx_size))
            where = (0,) * (at + 1) + (ty_at, ctx_at, 0)
        else:
            full = jnp.zeros(lead + (ctx_size, tz_size // ctx_size, ty_size, block), F32)
            own = values.reshape(lead + (1, tz_size // ctx_size, 1, block))
            where = (0,) * at + (ctx_at, 0, ty_at, 0)
        return lax.dynamic_update_slice(full, own, where).reshape(lead + (-1,))

    def flat(*values):
        return jnp.concatenate([one.reshape(-1, model) for one in values])

    summed_early = total(
        flat(
            jnp.sum(grad_final * normed_two, axis=0),
            jnp.sum(grad_final, axis=0),
            jnp.sum(grad_ffn.astype(F32), axis=0),
            jnp.sum(grad_hidden * normed_one, axis=0),
            jnp.sum(grad_hidden, axis=0),
            jnp.sum(grad_attended.astype(F32), axis=0),
            spread(jnp.sum(grad_pre.astype(F32), axis=0)),
        ),
        everywhere,
    )
    head_sums = jnp.sum(grad_heads.astype(F32), axis=0).reshape(heads, 3, HEAD)
    qv_sums = jnp.stack([head_sums[:, 0].reshape(-1), head_sums[:, 2].reshape(-1)])
    seq_slots = jnp.zeros((timesteps.shape[0], model), F32)
    seq_slots = lax.dynamic_update_index_in_dim(
        seq_slots, jnp.sum(grad_start, axis=0), sequence, 0
    )
    summed_late = total(flat(spread(qv_sums), seq_slots), everywhere)
    seq_sums = lax.dynamic_slice_in_dim(summed_late[2:], fsdp_at * part, part, 1)
    same_step = (timesteps[:, None] == timesteps[None, :]).astype(F32)
    step_rows = jnp.sum(same_step[:, :, None] * seq_sums[None], axis=1)
    grad_table = jnp.zeros((table.shape[0], part), F32)
    for one in range(timesteps.shape[0]):
        grad_table = lax.dynamic_update_slice(
            grad_table, step_rows[one : one + 1], (timesteps[one], 0)
        )
    pair = lambda first, second: jnp.stack([summed_early[first], summed_early[second]])
    return (
        output,
        grad_inputs,
        grad_table,
        red_qkv,
        summed_late[:2],
        red_out,
        red_up,
        summed_early[6:].reshape(-1),
        red_down,
        pair(5, 2),
        pair(3, 0),
        pair(4, 1),
    )


def solution(mesh):
    rows = P("fsdp", ("ctx", "tz", "ty"), None)
    tp = ("tz", "ty")
    in_specs = (
        rows,
        P(),
        P("fsdp", None),
        P(),
        P(None, "fsdp", tp),
        P(None, tp),
        P(tp, "fsdp"),
        P("fsdp", tp),
        P(tp),
        P(tp, "fsdp"),
        P(),
        P(),
        P(),
        rows,
    )
    out_specs = (
        rows,
        rows,
        P(None, "fsdp"),
        P(None, ("fsdp", "ctx"), tp),
        P(),
        P(tp, ("fsdp", "ctx")),
        P(("fsdp", "ctx"), tp),
        P(),
        P(tp, ("fsdp", "ctx")),
        P(),
        P(),
        P(),
    )

    def step(inputs, *rest):
        fsdp, ctx, tp_size = (mesh.shape[axis] for axis in ("fsdp", "ctx", "tp"))
        tz_size = inputs.shape[0] // fsdp
        devices = mesh.devices.reshape(fsdp, ctx, tz_size, tp_size // tz_size)
        split = Mesh(devices, ("fsdp", "ctx", "tz", "ty"))
        return jax.shard_map(
            shards, mesh=split, in_specs=in_specs, out_specs=out_specs, check_vma=False
        )(inputs, *rest)

    return step
```

```python
import jax
import jax.numpy as jnp
from jax import lax
from jax.experimental import pallas as pl
from jax.experimental.pallas import tpu as pltpu
from jax.sharding import Mesh
from jax.sharding import PartitionSpec as P

HEAD = 64
NORM_EPS = 1e-05
MASKED = -1e30
F32 = jnp.float32
BF16 = jnp.bfloat16
NN = ((1,), (0,))
NT = ((1,), (1,))
TN = ((0,), (0,))
LANES = 128
CHUNKS = 2
VMEM_BYTES = 60 << 20


def dot(left, right, dims):
    return lax.dot_general(left, right, (dims, ((), ())), preferred_element_type=F32)


def shape(rows, columns, dtype=BF16):
    return jax.ShapeDtypeStruct((rows, columns), dtype)


def kernel_call(body, outs, scalars, arrays, scratch=(), name=None):
    vmem = pl.BlockSpec(memory_space=pltpu.VMEM)
    smem = pl.BlockSpec(memory_space=pltpu.SMEM)
    return pl.pallas_call(
        body,
        out_shape=outs,
        in_specs=[smem] * len(scalars) + [vmem] * len(arrays),
        out_specs=[vmem] * len(outs),
        scratch_shapes=scratch,
        compiler_params=pltpu.CompilerParams(vmem_limit_bytes=VMEM_BYTES),
        name=name,
    )(*scalars, *arrays)


def project_qkv(at, own, away, step_row, bias, pieces):
    blocks, halves = len(pieces), len(pieces[0])
    half_rows, model = own.shape
    part = model // halves
    width = bias.shape[1]
    share = width // (3 * blocks)
    third = width // 3
    flat = [one for row in pieces for one in row]

    def body(at_ref, own_ref, away_ref, step_ref, bias_ref, *rest):
        piece_refs, (lowered_ref, qkv_ref, w_ref) = rest[: len(flat)], rest[len(flat) :]
        for block in range(blocks):
            for half in range(halves):
                piece = piece_refs[block * halves + half]
                for kind in range(3):
                    row = kind * third + block * share
                    w_ref[row : row + share, half * part : (half + 1) * part] = piece[
                        kind * share : (kind + 1) * share, :
                    ]
        count = TZ_STATIC[0]
        run = half_rows // count
        for which, ref in enumerate((own_ref, away_ref)):
            for rel in range(count):
                natural = lax.rem(at_ref[0] - rel + count, count)
                rows = (
                    ref[rel * run : (rel + 1) * run, :].astype(F32) + step_ref[...]
                ).astype(BF16)
                lowered_ref[pl.ds(which * half_rows + natural * run, run), :] = rows
        for first in range(0, 2 * half_rows, 256):
            rows = lowered_ref[first : first + 256, :]
            result = dot(rows, w_ref[...], NT) + bias_ref[...]
            qkv_ref[first : first + 256, :third] = (result[:, :third] * HEAD**-0.5).astype(BF16)
            qkv_ref[first : first + 256, third:] = result[:, third:].astype(BF16)

    return kernel_call(
        body,
        [shape(2 * half_rows, model), shape(2 * half_rows, width)],
        [at],
        [own, away, step_row, bias] + flat,
        [pltpu.VMEM((width, model), BF16)],
        "project_qkv",
    )


TZ_STATIC = [4]
BLOCK_Q = 128
BLOCK_K = 256


def active_blocks(docs):
    length = docs.shape[0]
    q_docs, k_docs = docs.reshape(-1, BLOCK_Q), docs.reshape(-1, BLOCK_K)
    active = (k_docs[None, :, 0] <= q_docs[:, None, -1]) & (k_docs[None, :, -1] >= q_docs[:, None, 0])
    active = active.astype(jnp.int32)
    blocks = length // BLOCK_K
    order = jnp.arange(blocks)
    place = jnp.sum(active[:, None, :] * (order[None, :] < order[:, None])[None], axis=2)
    hit = active[:, :, None] * (place[:, :, None] == order[None, None, :])
    listed = jnp.sum(hit * order[None, :, None], axis=1)
    return jnp.sum(active, axis=1), listed.reshape(-1)


def stacked(block):
    first = lax.broadcasted_iota(jnp.int32, block.shape, 1) < HEAD
    zero = jnp.zeros_like(block)
    return jnp.concatenate([jnp.where(first, block, zero), jnp.where(first, zero, block)])


def beside(pair):
    rows = pair.shape[0] // 2
    first = lax.broadcasted_iota(jnp.int32, (rows, LANES), 1) < HEAD
    return jnp.where(first, pair[:rows], pair[rows:])


def attend(counts, listed, qkv, docs_column, docs_row):
    length, width = qkv.shape
    pairs = width // (3 * LANES)
    key_blocks = length // BLOCK_K

    def body(counts_ref, listed_ref, q_ref, k_ref, v_ref, column_ref, row_ref, o_ref, lse_ref, s_ref):
        at = pl.program_id(1)
        count = counts_ref[at]
        query = stacked(q_ref[...])
        column = column_ref[...]
        column = jnp.concatenate([column, column])

        def find(step, peak):
            block = listed_ref[at * key_blocks + step]
            rows = pl.ds(pl.multiple_of(block * BLOCK_K, BLOCK_K), BLOCK_K)
            scores = dot(query, k_ref[rows, :], NT)
            scores = jnp.where(column == row_ref[block], scores, MASKED)
            s_ref[step] = scores
            for lane in range(0, BLOCK_K, LANES):
                peak = jnp.maximum(peak, scores[:, lane : lane + LANES])
            return peak

        peak = lax.fori_loop(0, count, find, jnp.full((2 * BLOCK_Q, LANES), MASKED, F32))
        peak = jnp.max(peak, axis=1, keepdims=True)

        def gather(step, carry):
            total, mixed = carry
            block = listed_ref[at * key_blocks + step]
            rows = pl.ds(pl.multiple_of(block * BLOCK_K, BLOCK_K), BLOCK_K)
            weights = jnp.exp(s_ref[step] - peak)
            for lane in range(0, BLOCK_K, LANES):
                total = total + weights[:, lane : lane + LANES]
            return total, mixed + dot(weights.astype(BF16), v_ref[rows, :], NN)

        zero = jnp.zeros((2 * BLOCK_Q, LANES), F32)
        total, mixed = lax.fori_loop(0, count, gather, (zero, zero))
        total = jnp.sum(total, axis=1, keepdims=True)
        o_ref[...] = beside(mixed / total).astype(BF16)
        lse_ref[...] = beside(jnp.broadcast_to(peak + jnp.log(total), (2 * BLOCK_Q, LANES)))

    grid_spec = pltpu.PrefetchScalarGridSpec(
        num_scalar_prefetch=2,
        grid=(pairs, length // BLOCK_Q),
        in_specs=[
            pl.BlockSpec((BLOCK_Q, LANES), lambda pair, q, *_: (q, pair)),
            pl.BlockSpec((length, LANES), lambda pair, q, *_: (0, pairs + pair)),
            pl.BlockSpec((length, LANES), lambda pair, q, *_: (0, 2 * pairs + pair)),
            pl.BlockSpec((BLOCK_Q, 1), lambda pair, q, *_: (q, 0)),
            pl.BlockSpec(docs_row.shape, lambda pair, q, *_: (0, 0, 0)),
        ],
        out_specs=[pl.BlockSpec((BLOCK_Q, LANES), lambda pair, q, *_: (q, pair))] * 2,
        scratch_shapes=[pltpu.VMEM((key_blocks, 2 * BLOCK_Q, BLOCK_K), F32)],
    )
    return pl.pallas_call(
        body,
        out_shape=[shape(length, pairs * LANES), shape(length, pairs * LANES, F32)],
        grid_spec=grid_spec,
        compiler_params=pltpu.CompilerParams(vmem_limit_bytes=VMEM_BYTES),
        name="attend",
    )(counts, listed, qkv, qkv, qkv, docs_column, docs_row)


def attend_back(counts, listed, qkv, grad_mixed, mixed, lse, docs_column, docs_row):
    length, width = qkv.shape
    pairs = width // (3 * LANES)
    key_blocks = length // BLOCK_K
    last = length // BLOCK_Q - 1

    def body(
        counts_ref, listed_ref, q_ref, k_ref, v_ref, g_ref, o_ref, lse_ref, column_ref, row_ref,
        dq_ref, dk_ref, dv_ref, dk_sum, dv_sum,
    ):
        at = pl.program_id(1)

        @pl.when(at == 0)
        def _():
            dk_sum[...] = jnp.zeros_like(dk_sum)
            dv_sum[...] = jnp.zeros_like(dv_sum)

        query = stacked(q_ref[...])
        grad = stacked(g_ref[...])
        out = o_ref[...].astype(F32)
        row_dot = jnp.sum(grad.astype(F32) * jnp.concatenate([out, out]), axis=1, keepdims=True)
        column = column_ref[...]
        column = jnp.concatenate([column, column])
        lse_pair = lse_ref[...]
        log_total = jnp.concatenate([lse_pair[:, :1], lse_pair[:, HEAD : HEAD + 1]])

        def one(step, dq):
            block = listed_ref[at * key_blocks + step]
            rows = pl.ds(pl.multiple_of(block * BLOCK_K, BLOCK_K), BLOCK_K)
            key, value = k_ref[rows, :], v_ref[rows, :]
            scores = dot(query, key, NT)
            scores = jnp.where(column == row_ref[block], scores, MASKED)
            weights = jnp.exp(scores - log_total)
            grad_weights = dot(grad, value, NT)
            grad_scores = (weights * (grad_weights - row_dot)).astype(BF16)
            dv_sum[rows, :] += dot(weights.astype(BF16), grad, TN)
            dk_sum[rows, :] += dot(grad_scores, query, TN)
            return dq + dot(grad_scores, key, NN)

        dq = lax.fori_loop(0, counts_ref[at], one, jnp.zeros((2 * BLOCK_Q, LANES), F32))
        dq_ref[...] = (beside(dq) * HEAD**-0.5).astype(BF16)

        @pl.when(at == last)
        def _():
            dk_ref[...] = dk_sum[...].astype(BF16)
            dv_ref[...] = dv_sum[...].astype(BF16)

    block = pl.BlockSpec((BLOCK_Q, LANES), lambda pair, q, *_: (q, pair))
    whole = pl.BlockSpec((length, LANES), lambda pair, q, *_: (0, pair))
    grid_spec = pltpu.PrefetchScalarGridSpec(
        num_scalar_prefetch=2,
        grid=(pairs, length // BLOCK_Q),
        in_specs=[
            block,
            pl.BlockSpec((length, LANES), lambda pair, q, *_: (0, pairs + pair)),
            pl.BlockSpec((length, LANES), lambda pair, q, *_: (0, 2 * pairs + pair)),
            block,
            block,
            block,
            pl.BlockSpec((BLOCK_Q, 1), lambda pair, q, *_: (q, 0)),
            pl.BlockSpec(docs_row.shape, lambda pair, q, *_: (0, 0, 0)),
        ],
        out_specs=[block, whole, whole],
        scratch_shapes=[pltpu.VMEM((length, LANES), F32)] * 2,
    )
    return pl.pallas_call(
        body,
        out_shape=[shape(length, pairs * LANES)] * 3,
        grid_spec=grid_spec,
        compiler_params=pltpu.CompilerParams(vmem_limit_bytes=VMEM_BYTES),
        name="attend_back",
    )(counts, listed, qkv, qkv, qkv, grad_mixed, mixed, lse, docs_column, docs_row)


def join_weights(pieces, heights):
    blocks, halves = len(pieces), len(pieces[0])
    part = pieces[0][0].shape[1]
    flat = [one for row in pieces for one in row]

    def body(*refs):
        ins, outs, sem = refs[: len(flat)], refs[len(flat) : -1], refs[-1]
        copies = []
        first = 0
        for out, height in zip(outs, heights):
            for block in range(blocks):
                for half in range(halves):
                    copies.append(
                        pltpu.make_async_copy(
                            ins[block * halves + half].at[first : first + height, :],
                            out.at[
                                block * height : (block + 1) * height,
                                half * part : (half + 1) * part,
                            ],
                            sem.at[len(copies)],
                        )
                    )
            first += height
        for one in copies:
            one.start()
        for one in copies:
            one.wait()

    hbm = pl.BlockSpec(memory_space=pl.ANY)
    return pl.pallas_call(
        body,
        out_shape=[shape(blocks * height, halves * part) for height in heights],
        in_specs=[hbm] * len(flat),
        out_specs=[hbm] * len(heights),
        scratch_shapes=[pltpu.SemaphoreType.DMA((len(flat) * len(heights),))],
        name="join_weights",
    )(*flat)


def token_rows(ref, first, chunk, at, count, run):
    per = count // CHUNKS
    rows = []
    for rel in range(chunk * per, (chunk + 1) * per):
        natural = lax.rem(at - rel + count, count)
        rows.append(ref[pl.ds(first + natural * run, run), :])
    return jnp.concatenate(rows)


def project_out(at, mixed, weight):
    length, model = mixed.shape[0], weight.shape[1]
    half_rows = length // 2
    rows = half_rows // CHUNKS

    def body(at_ref, mixed_ref, w_ref, *outs):
        count = TZ_STATIC[0]
        for chunk in range(CHUNKS):
            for which in range(2):
                part = token_rows(mixed_ref, which * half_rows, chunk, at_ref[0], count, half_rows // count)
                result = dot(part, w_ref[...], NN)
                out = outs[chunk * 2 + which]
                out[...] = result.astype(out.dtype)

    return kernel_call(
        body,
        [shape(rows, model, F32), shape(rows, model)] * CHUNKS,
        [at],
        [mixed, weight],
        (),
        "project_out",
    )


def feed_forward(own, away, bias, up, down):
    rows, model = own.shape
    hidden = up.shape[0]
    step = 256

    def body(own_ref, away_ref, bias_ref, up_ref, down_ref, sum_ref, send_ref, act_ref, slope_ref, in_ref):
        in_ref[:rows, :] = own_ref[...]
        in_ref[rows:, :] = away_ref[...]
        for first in range(0, hidden, step):
            cut = slice(first, first + step)
            pre = dot(in_ref[...], up_ref[cut, :], NT) + bias_ref[:, cut]
            cdf = 0.5 * (1.0 + lax.erf(pre * (0.5**0.5)))
            act_ref[:, cut] = (pre * cdf).astype(BF16)
            density = jnp.exp(-0.5 * pre * pre) * (0.5 / jnp.pi) ** 0.5
            slope_ref[:, cut] = (cdf + pre * density).astype(BF16)
        send_ref[...] = dot(act_ref[rows:, :], down_ref[...], NN).astype(BF16)
        sum_ref[...] = dot(act_ref[:rows, :], down_ref[...], NN)

    return kernel_call(
        body,
        [shape(rows, model, F32), shape(rows, model), shape(2 * rows, hidden), shape(2 * rows, hidden)],
        [],
        [own, away, bias, up, down],
        [pltpu.VMEM((2 * rows, model), BF16)],
        "feed_forward",
    )


def feed_back(own, away, slope, up, down):
    rows, model = own.shape
    hidden = up.shape[0]
    step = 256

    def body(own_ref, away_ref, slope_ref, up_ref, down_ref, sum_ref, send_ref, pre_ref, total_ref, in_ref):
        in_ref[:rows, :] = own_ref[...]
        in_ref[rows:, :] = away_ref[...]
        for first in range(0, hidden, step):
            cut = slice(first, first + step)
            grad = dot(in_ref[...], down_ref[cut, :], NT) * slope_ref[:, cut].astype(F32)
            low = grad.astype(BF16)
            pre_ref[:, cut] = low
            total_ref[:, cut] = jnp.sum(low.astype(F32), axis=0, keepdims=True)
        send_ref[...] = dot(pre_ref[rows:, :], up_ref[...], NN).astype(BF16)
        sum_ref[...] = dot(pre_ref[:rows, :], up_ref[...], NN)

    return kernel_call(
        body,
        [shape(rows, model, F32), shape(rows, model), shape(2 * rows, hidden), shape(1, hidden, F32)],
        [],
        [own, away, slope, up, down],
        [pltpu.VMEM((2 * rows, model), BF16)],
        "feed_back",
    )


def weight_grad(lefts, rights, halves, name):
    rows, height = lefts[0].shape
    model = rights[0][0].shape[1]
    part = model // halves
    step = 256 if height % 256 == 0 else height
    flat = [one for chunk in rights for one in chunk]

    def body(*refs):
        left_refs = refs[: len(lefts)]
        right_refs = refs[len(lefts) : len(lefts) + len(flat)]
        outs = refs[len(lefts) + len(flat) : -1]
        all_ref = refs[-1]

        @pl.when(pl.program_id(0) == 0)
        def _():
            first = 0
            for ref in right_refs:
                all_ref[first : first + ref.shape[0], :] = ref[...]
                first += ref.shape[0]

        result = None
        for index, ref in enumerate(left_refs):
            term = dot(ref[...], all_ref[index * rows : (index + 1) * rows, :], TN)
            result = term if result is None else result + term
        for half, out in enumerate(outs):
            out[...] = result[:, half * part : (half + 1) * part].astype(BF16)

    return pl.pallas_call(
        body,
        out_shape=[shape(height, part)] * halves,
        grid=(height // step,),
        in_specs=[pl.BlockSpec((rows, step), lambda at: (0, at))] * len(lefts)
        + [pl.BlockSpec(one.shape, lambda at: (0, 0)) for one in flat],
        out_specs=[pl.BlockSpec((step, part), lambda at: (at, 0))] * halves,
        scratch_shapes=[pltpu.VMEM((rows * len(lefts), model), BF16)],
        compiler_params=pltpu.CompilerParams(vmem_limit_bytes=VMEM_BYTES),
        name=name,
    )(*lefts, *flat)


def mixed_grads(at, owns, aways, mixed, weight, halves):
    length, width = mixed.shape
    model = weight.shape[1]
    part = model // halves
    half_rows = length // 2
    per = half_rows // CHUNKS

    def body(at_ref, *refs):
        own_refs, away_refs = refs[:CHUNKS], refs[CHUNKS : 2 * CHUNKS]
        mixed_ref, w_ref = refs[2 * CHUNKS : 2 * CHUNKS + 2]
        grad_ref = refs[2 * CHUNKS + 2]
        outs, all_ref = refs[2 * CHUNKS + 3 : -1], refs[-1]
        count = TZ_STATIC[0]
        run = half_rows // count
        for which, group in enumerate((own_refs, away_refs)):
            for rel in range(count):
                natural = lax.rem(at_ref[0] - rel + count, count)
                ref = group[rel * run // per]
                first = rel * run % per
                all_ref[pl.ds(which * half_rows + natural * run, run), :] = ref[first : first + run, :]
        for first in range(0, length, 256):
            cut = slice(first, first + 256)
            grad_ref[cut, :] = dot(all_ref[cut, :], w_ref[...], NT).astype(BF16)
        result = dot(mixed_ref[...], all_ref[...], TN)
        for half, out in enumerate(outs):
            out[...] = result[:, half * part : (half + 1) * part].astype(BF16)

    return kernel_call(
        body,
        [shape(length, width)] + [shape(width, part)] * halves,
        [at],
        [*owns, *aways, mixed, weight],
        [pltpu.VMEM((length, model), BF16)],
        "mixed_grads",
    )


def return_rows(at, grads, pieces):
    length, third = grads[0].shape
    blocks, halves = len(pieces), len(pieces[0])
    part = pieces[0][0].shape[1]
    model = part * halves
    share = third // blocks
    half_rows = length // 2
    flat = [one for row in pieces for one in row]

    def body(at_ref, q_ref, k_ref, v_ref, *rest):
        piece_refs, (sum_ref, send_ref, total_ref, w_ref) = rest[: len(flat)], rest[len(flat) :]
        for block in range(blocks):
            for half in range(halves):
                piece = piece_refs[block * halves + half]
                for kind in range(3):
                    row = kind * third + block * share
                    w_ref[row : row + share, half * part : (half + 1) * part] = piece[
                        kind * share : (kind + 1) * share, :
                    ]
        count = TZ_STATIC[0]
        run = half_rows // count
        per = half_rows // CHUNKS
        for which, out in ((1, send_ref), (0, sum_ref)):
            for chunk in range(CHUNKS):
                result = None
                for kind, ref in enumerate((q_ref, k_ref, v_ref)):
                    rows = token_rows(ref, which * half_rows, chunk, at_ref[0], count, run)
                    term = dot(rows, w_ref[kind * third : (kind + 1) * third, :], NN)
                    result = term if result is None else result + term
                out[chunk * per : (chunk + 1) * per, :] = result.astype(out.dtype)
        for kind, ref in enumerate((q_ref, k_ref, v_ref)):
            total_ref[:, kind * third : (kind + 1) * third] = jnp.sum(
                ref[...].astype(F32), axis=0, keepdims=True
            )

    return kernel_call(
        body,
        [shape(half_rows, model, F32), shape(half_rows, model), shape(1, 3 * third, F32)],
        [at],
        [*grads, *flat],
        [pltpu.VMEM((3 * third, model), BF16)],
        "return_rows",
    )


def place_rows(zeros, steps, tiles):
    count = steps.shape[0]

    def body(steps_ref, tiles_ref, zeros_ref, out_ref, sem):
        del zeros_ref
        copies = [
            pltpu.make_async_copy(
                tiles_ref.at[8 * one : 8 * one + 8, :],
                out_ref.at[pl.ds(pl.multiple_of(steps_ref[one] // 8 * 8, 8), 8), :],
                sem.at[one],
            )
            for one in range(count)
        ]
        for one in copies:
            one.start()
        for one in copies:
            one.wait()

    return pl.pallas_call(
        body,
        out_shape=jax.ShapeDtypeStruct(zeros.shape, zeros.dtype),
        in_specs=[
            pl.BlockSpec(memory_space=pltpu.SMEM),
            pl.BlockSpec(memory_space=pltpu.VMEM),
            pl.BlockSpec(memory_space=pl.ANY),
        ],
        out_specs=pl.BlockSpec(memory_space=pl.ANY),
        scratch_shapes=[pltpu.SemaphoreType.DMA((count,))],
        input_output_aliases={2: 0},
        name="place_rows",
    )(steps, tiles, zeros)


def swap(rows, axis):
    return lax.ppermute(rows, axis, [(0, 1), (1, 0)])


def pick(parts, index, at):
    return lax.dynamic_index_in_dim(parts, index, at, keepdims=False)


def join(*values):
    return lax.optimization_barrier(values)


def norm(rows):
    centered = rows - jnp.mean(rows, axis=-1, keepdims=True)
    inverse = lax.rsqrt(jnp.mean(centered * centered, axis=-1, keepdims=True) + NORM_EPS)
    return centered * inverse, inverse


def norm_back(normed, inverse, gain, grad):
    scaled = grad * gain
    mean_one = jnp.mean(scaled, axis=-1, keepdims=True)
    mean_two = jnp.mean(scaled * normed, axis=-1, keepdims=True)
    return (scaled - mean_one - normed * mean_two) * inverse


def total(values, axes):
    for axis in axes:
        size = lax.axis_size(axis)
        if size & (size - 1):
            values = lax.psum(values, axis)
            continue
        step = 1
        while step < size:
            values = values + lax.ppermute(values, axis, [(one, one ^ step) for one in range(size)])
            step *= 2
    return values


def shards(
    inputs,
    timesteps,
    segments,
    table,
    w_qkv,
    qv_bias,
    w_out,
    w_up,
    ffn_bias,
    w_down,
    out_biases,
    norm_gains,
    norm_biases,
    cotangent,
):
    fsdp_size, ctx_size = lax.axis_size("fsdp"), lax.axis_size("ctx")
    tz_size, ty_size = lax.axis_size("tz"), lax.axis_size("ty")
    fsdp_at, ctx_at = lax.axis_index("fsdp"), lax.axis_index("ctx")
    tz_at, ty_at = lax.axis_index("tz"), lax.axis_index("ty")
    TZ_STATIC[0] = tz_size
    seq_here, piece, model = inputs.shape
    length = segments.shape[1]
    part = model // fsdp_size
    half_rows = length // ctx_size
    chunk_rows = half_rows // CHUNKS
    run = ty_size * piece
    block_heads = w_qkv.shape[2] // HEAD
    cut = block_heads % ctx_size == 0
    blocks = tz_size if cut else tz_size // ctx_size

    def shift(core, block):
        return block if cut else core * blocks + block

    def ring(block, sign):
        return [
            (core * tz_size + z, core * tz_size + (z + sign * shift(core, block)) % tz_size)
            for core in range(ctx_size)
            for z in range(tz_size)
        ]

    def along(values, block, sign):
        if cut and block == 0:
            return values
        return lax.ppermute(values, ("ctx", "tz"), ring(block, sign))

    def halves_order(values):
        if fsdp_size != 2:
            return values
        turned = jnp.concatenate([values[..., part:], values[..., :part]], axis=-1)
        return jnp.where(fsdp_at == 0, values, turned)

    def across(values):
        if fsdp_size == 2:
            return [values, swap(values, "fsdp")]
        gathered = lax.all_gather(values, "fsdp", axis=0, tiled=False)
        return [gathered[one] for one in range(fsdp_size)]

    def share(values):
        if not cut:
            return values
        return pick(values.reshape((ctx_size, -1) + values.shape[1:]), ctx_at, 0)

    turned = jnp.transpose(w_qkv, (0, 2, 1))
    if cut:
        turned = pick(turned.reshape(3, ctx_size, -1, part), ctx_at, 1)
    qkv_rows = turned.reshape(-1, part)
    third = qkv_rows.shape[0] // 3
    qv_share = pick(qv_bias.reshape(2, ctx_size, -1), ctx_at, 1) if cut else qv_bias
    ffn_share = share(ffn_bias)
    bias_flat = jnp.concatenate([qv_share.reshape(-1), ffn_share])
    bias_rows = -(-bias_flat.shape[0] // (16 * part)) * 16
    bias_block = jnp.pad(bias_flat, (0, bias_rows * part - bias_flat.shape[0])).reshape(-1, part)
    first_block = jnp.concatenate([qkv_rows, bias_block])
    rest_block = jnp.concatenate([share(w_out), share(w_up.T), share(w_down)])
    out_height = w_out.shape[0] // (ctx_size if cut else 1)
    hidden_height = ffn_share.shape[0]

    first_pieces = [across(along(first_block, block, 1)) for block in range(blocks)]

    def arrive(values):
        got = [pick(values, tz_at, 0)]
        for step in range(1, tz_size):
            sent = pick(values, (tz_at + step) % tz_size, 0)
            got.append(lax.ppermute(sent, "tz", [(z, (z + step) % tz_size) for z in range(tz_size)]))
        return jnp.stack(got)

    def depart(values):
        values = values.reshape(tz_size, piece, model)
        result = jnp.zeros_like(values)
        for step in range(tz_size):
            got = values[step]
            if step:
                got = lax.ppermute(got, "tz", [(z, (z - step) % tz_size) for z in range(tz_size)])
            result = lax.dynamic_update_index_in_dim(result, got, (tz_at + step) % tz_size, 0)
        return result

    def over_y(values):
        if ty_size != 2:
            return lax.all_gather(values, "ty", axis=1, tiled=False)
        own = (jnp.arange(2) == ty_at).reshape(1, 2, 1, 1)
        return jnp.where(own, values[:, None], swap(values, "ty")[:, None])

    def half_of(values):
        return over_y(arrive(halves_order(values))).reshape(half_rows, model)

    own_inputs = half_of(inputs)
    away_inputs = swap(own_inputs, "ctx")
    own_grad = half_of(cotangent)
    rest_pieces = [across(along(rest_block, block, 1)) for block in range(blocks)]

    biases = [row[0][3 * third :].reshape(-1)[: bias_flat.shape[0]].astype(F32) for row in first_pieces]
    q_bias = jnp.concatenate([one[:third] for one in biases])
    v_bias = jnp.concatenate([one[third : 2 * third] for one in biases])
    qkv_bias = jnp.concatenate([q_bias, jnp.zeros_like(q_bias), v_bias])[None]
    hidden_bias = jnp.concatenate([one[2 * third :] for one in biases])[None]
    biases_out = halves_order(out_biases.astype(F32))
    gains = halves_order(norm_gains.astype(F32))
    offsets = halves_order(norm_biases.astype(F32))

    sequence = fsdp_at * seq_here + tz_at
    docs = pick(segments, tz_at, 0).reshape(ctx_size, half_rows)
    docs = jnp.concatenate([pick(docs, ctx_at, 0), pick(docs, 1 - ctx_at, 0)])
    docs_column, docs_row = docs[:, None], docs.reshape(-1, 1, BLOCK_K)
    counts, listed = active_blocks(docs)
    step_row = halves_order(lax.dynamic_slice_in_dim(table, timesteps[sequence], 1, 0).astype(F32))
    at = jnp.stack([tz_at, ty_at]).astype(jnp.int32)

    zero_table = jnp.zeros((table.shape[0], part), F32)
    own_inputs, zero_table = join(own_inputs, zero_table)

    lowered, qkv = project_qkv(at, own_inputs, away_inputs, step_row, qkv_bias, first_pieces)
    mixed, lse = attend(counts, listed, qkv, docs_column, docs_row)
    out_all, up_all, down_all = join_weights(rest_pieces, [out_height, hidden_height, hidden_height])
    start = own_inputs.astype(F32) + step_row

    def reduce_rows(own, send):
        summed = (own + swap(send, "ctx").astype(F32)).astype(BF16)
        if ty_size != 2:
            return lax.psum(summed.astype(F32), "ty")
        return summed.astype(F32) + swap(summed, "ty").astype(F32)

    def rows_of(values, chunk):
        return values[chunk * chunk_rows : (chunk + 1) * chunk_rows]

    partials = project_out(at, mixed, out_all)
    every = range(CHUNKS)
    normed_one, inverse_one, hidden, hidden_own, hidden_away = [], [], [], [], []
    for chunk in every:
        attended = reduce_rows(partials[2 * chunk], partials[2 * chunk + 1]) + biases_out[0]
        normed, inverse = norm(rows_of(start, chunk) + attended)
        normed_one.append(normed)
        inverse_one.append(inverse)
        hidden.append(normed * gains[0] + offsets[0])
        hidden_own.append(hidden[-1].astype(BF16))
        hidden_away.append(swap(hidden_own[-1], "ctx"))
    forward = [
        feed_forward(hidden_own[chunk], hidden_away[chunk], hidden_bias, up_all, down_all)
        for chunk in every
    ]
    outputs, normed_two, grad_final, grad_second, ffn_own, ffn_away = [], [], [], [], [], []
    for chunk in every:
        ffn_out = reduce_rows(forward[chunk][0], forward[chunk][1]) + biases_out[1]
        normed, inverse = norm(hidden[chunk] + ffn_out)
        normed_two.append(normed)
        outputs.append((normed * gains[1] + offsets[1]).astype(BF16))
        grad_final.append(rows_of(own_grad, chunk).astype(F32))
        grad_second.append(norm_back(normed, inverse, gains[1], grad_final[-1]))
        ffn_own.append(grad_second[-1].astype(BF16))
        ffn_away.append(swap(ffn_own[-1], "ctx"))
    activated = [one[2] for one in forward]
    backward = [
        feed_back(ffn_own[chunk], ffn_away[chunk], forward[chunk][3], up_all, down_all)
        for chunk in every
    ]
    grad_pre = [one[2] for one in backward]
    grad_down = weight_grad(activated, list(zip(ffn_own, ffn_away)), fsdp_size, "down_grad")
    grad_up = weight_grad(grad_pre, list(zip(hidden_own, hidden_away)), fsdp_size, "up_grad")
    grad_hidden, grad_first, first_own, first_away = [], [], [], []
    for chunk in every:
        grad_hidden.append(grad_second[chunk] + reduce_rows(backward[chunk][0], backward[chunk][1]))
        grad_first.append(norm_back(normed_one[chunk], inverse_one[chunk], gains[0], grad_hidden[-1]))
        first_own.append(grad_first[-1].astype(BF16))
        first_away.append(swap(first_own[-1], "ctx"))
    grad_mixed, *grad_out = mixed_grads(at, first_own, first_away, mixed, out_all, fsdp_size)
    grads = attend_back(counts, listed, qkv, grad_mixed, mixed, lse, docs_column, docs_row)
    start_own, start_send, head_sums = return_rows(at, grads, first_pieces)
    grad_qkv = [
        weight_grad([one], [(lowered,)], fsdp_size, "qkv_grad") for one in grads
    ]
    grad_qkv = [jnp.concatenate([one[half] for one in grad_qkv]) for half in range(fsdp_size)]

    def own_y(values):
        return pick(values.reshape(tz_size, ty_size, piece, model), ty_at, 1)

    output = halves_order(depart(own_y(jnp.concatenate(outputs))))

    summed = start_own + swap(start_send, "ctx").astype(F32)
    if ty_size == 2:
        grid = summed.reshape(tz_size, 2, piece, model)
        returned = pick(grid, ty_at, 1) + swap(pick(grid, 1 - ty_at, 1).astype(BF16), "ty").astype(F32)
    else:
        grid = summed.astype(BF16).reshape(tz_size, ty_size, piece, model)
        returned = lax.psum_scatter(grid, "ty", scatter_dimension=1, tiled=False).astype(F32)
    grad_start = own_y(jnp.concatenate(grad_first)) + returned
    grad_inputs = halves_order(depart(grad_start.astype(BF16)))

    def over_x(grads):
        if fsdp_size == 2:
            return (grads[0].astype(F32) + swap(grads[1], "fsdp").astype(F32)).astype(BF16)
        return lax.psum_scatter(jnp.stack(grads), "fsdp", scatter_dimension=0, tiled=False)

    def release(grads, kinds):
        summed = over_x(grads).reshape(kinds, blocks, -1, part)
        own = None
        for block in range(blocks):
            got = along(summed[:, block], block, -1).astype(F32)
            own = got if own is None else own + got
        pieces = own.reshape(own.shape[:-1] + (ctx_size, -1))
        kept = pick(pieces, ctx_at, 2)
        away = swap(pick(pieces, 1 - ctx_at, 2).astype(BF16), "ctx").astype(F32)
        if not cut:
            return kept + away
        order = (jnp.arange(2) == ctx_at)[None, :, None, None]
        both = jnp.where(order, kept[:, None], away[:, None])
        return both.reshape(kinds, -1, both.shape[-1])

    red_down = release(grad_down, 1)[0]
    red_up = release(grad_up, 1)[0].T
    red_out = release(grad_out, 1)[0]
    red_qkv = jnp.transpose(release(grad_qkv, 3), (0, 2, 1))

    def spread(values):
        kinds, _, width = values.shape
        if cut:
            full = jnp.zeros((kinds, tz_size, ty_size, ctx_size, width), F32)
        else:
            full = jnp.zeros((kinds, tz_size, ty_size, 1, width), F32)
        core = ctx_at if cut else 0
        for block in range(blocks):
            away = block if cut else ctx_at * blocks + block
            full = lax.dynamic_update_slice(
                full,
                values[:, block].reshape(kinds, 1, 1, 1, width),
                (0, (tz_at - away) % tz_size, ty_at, core, 0),
            )
        return full.reshape(kinds, -1)

    def rows_sum(values):
        return sum(jnp.sum(one.astype(F32), axis=0) for one in values)

    once = (ty_at == 0).astype(F32)
    row_sums = once * halves_order(
        jnp.stack(
            [
                rows_sum([a * b for a, b in zip(grad_hidden, normed_one)]),
                rows_sum([a * b for a, b in zip(grad_final, normed_two)]),
                rows_sum(grad_hidden),
                rows_sum(grad_final),
                rows_sum(first_own),
                rows_sum(ffn_own),
                rows_sum(grad_first),
            ]
        )
    )
    heads = head_sums.reshape(3, blocks, -1)
    first_cut = lax.reduce_precision(head_sums, 8, 7)
    second_cut = lax.reduce_precision(head_sums - first_cut, 8, 7)
    third_cut = head_sums - first_cut - second_cut
    split = jnp.concatenate([first_cut, second_cut, third_cut]).astype(BF16)
    seq_sum = 0.0
    for block in range(blocks):
        own_columns = split.reshape(3, 3, blocks, -1)[:, :, block].reshape(3, -1)
        seq_sum = seq_sum + jnp.concatenate(
            [
                jnp.sum(dot(own_columns, one[: 3 * third], NN), axis=0)
                for one in first_pieces[block]
            ]
        )
    seq_sum = halves_order(seq_sum) + row_sums[6]
    slots = jnp.zeros((timesteps.shape[0], model), F32)
    slots = lax.dynamic_update_index_in_dim(slots, seq_sum, sequence, 0)
    sums = total(
        jnp.concatenate(
            [
                row_sums[:6],
                spread(heads[::2]),
                spread(sum(one[3] for one in backward).reshape(1, blocks, -1)).reshape(-1, model),
                slots,
            ]
        ),
        ("ctx", "ty", "fsdp", "tz"),
    )
    hidden_rows = tz_size * ty_size * hidden_height * (ctx_size if cut else 1) // model
    seq_sums = lax.dynamic_slice_in_dim(sums[8 + hidden_rows :], fsdp_at * part, part, 1)
    tile_rows = (timesteps // 8 * 8)[:, None] + jnp.arange(8)[None]
    match = (tile_rows[:, :, None] == timesteps[None, None, :]).astype(F32)
    tiles = jnp.sum(match[..., None] * seq_sums[None, None], axis=2).reshape(-1, part)
    grad_table = place_rows(zero_table, timesteps, tiles)
    return (
        output,
        grad_inputs,
        grad_table,
        red_qkv,
        sums[6:8],
        red_out,
        red_up,
        sums[8 : 8 + hidden_rows].reshape(-1),
        red_down,
        sums[4:6],
        sums[:2],
        sums[2:4],
    )


def solution(mesh):
    rows = P("fsdp", ("ctx", "tz", "ty"), None)
    tp = ("tz", "ty")
    in_specs = (
        rows,
        P(),
        P("fsdp", None),
        P(),
        P(None, "fsdp", tp),
        P(None, tp),
        P(tp, "fsdp"),
        P("fsdp", tp),
        P(tp),
        P(tp, "fsdp"),
        P(),
        P(),
        P(),
        rows,
    )
    out_specs = (
        rows,
        rows,
        P(None, "fsdp"),
        P(None, ("fsdp", "ctx"), tp),
        P(),
        P(tp, ("fsdp", "ctx")),
        P(("fsdp", "ctx"), tp),
        P(),
        P(tp, ("fsdp", "ctx")),
        P(),
        P(),
        P(),
    )

    def step(inputs, *rest):
        fsdp, ctx, tp_size = (mesh.shape[axis] for axis in ("fsdp", "ctx", "tp"))
        tz_size = inputs.shape[0] // fsdp
        devices = mesh.devices.reshape(fsdp, ctx, tz_size, tp_size // tz_size)
        split = Mesh(devices, ("fsdp", "ctx", "tz", "ty"))
        return jax.shard_map(
            shards, mesh=split, in_specs=in_specs, out_specs=out_specs, check_vma=False
        )(inputs, *rest)

    return step
```

```python
import jax
import jax.numpy as jnp
from jax import lax
from jax.experimental import pallas as pl
from jax.experimental.pallas import tpu as pltpu
from jax.sharding import Mesh
from jax.sharding import PartitionSpec as P

HEAD = 64
NORM_EPS = 1e-05
MASKED = -1e30
F32 = jnp.float32
BF16 = jnp.bfloat16
NN = ((1,), (0,))
NT = ((1,), (1,))
TN = ((0,), (0,))
LANES = 128
CHUNKS = 2
VMEM_BYTES = 60 << 20


def dot(left, right, dims):
    return lax.dot_general(left, right, (dims, ((), ())), preferred_element_type=F32)


def shape(rows, columns, dtype=BF16):
    return jax.ShapeDtypeStruct((rows, columns), dtype)


def cost(flops, arrays):
    moved = sum(one.size * one.dtype.itemsize for one in arrays)
    return pl.CostEstimate(flops=int(flops), transcendentals=0, bytes_accessed=int(moved))


def params():
    return pltpu.CompilerParams(vmem_limit_bytes=VMEM_BYTES)


def kernel_call(body, outs, scalars, arrays, scratch, flops, name):
    vmem = pl.BlockSpec(memory_space=pltpu.VMEM)
    smem = pl.BlockSpec(memory_space=pltpu.SMEM)
    return pl.pallas_call(
        body,
        out_shape=outs,
        in_specs=[smem] * len(scalars) + [vmem] * len(arrays),
        out_specs=[vmem] * len(outs),
        scratch_shapes=scratch,
        compiler_params=params(),
        cost_estimate=cost(flops, [*arrays, *outs]),
        name=name,
    )(*scalars, *arrays)


def assemble(piece_refs, blocks, halves, part, first, share, kinds, w_ref):
    for block in range(blocks):
        for half in range(halves):
            piece = piece_refs[block * halves + half]
            for kind in range(kinds):
                row = (kind * blocks + block) * share
                start = first + kind * share
                w_ref[row : row + share, half * part : (half + 1) * part] = piece[
                    start : start + share, :
                ]


def project_qkv(at, own, away, step_row, bias, pieces, count):
    blocks, halves = len(pieces), len(pieces[0])
    half_rows, model = own.shape
    part = model // halves
    width = bias.shape[1]
    third = width // 3
    flat = [one for row in pieces for one in row]

    def body(at_ref, own_ref, away_ref, step_ref, bias_ref, *rest):
        piece_refs, (lowered_ref, qkv_ref, w_ref) = rest[: len(flat)], rest[len(flat) :]
        assemble(piece_refs, blocks, halves, part, 0, third // blocks, 3, w_ref)
        run = half_rows // count
        for which, ref in enumerate((own_ref, away_ref)):
            for rel in range(count):
                natural = lax.rem(at_ref[0] - rel + count, count)
                rows = ref[rel * run : (rel + 1) * run, :].astype(F32) + step_ref[...]
                place = pl.multiple_of(which * half_rows + natural * run, run)
                lowered_ref[pl.ds(place, run), :] = rows.astype(BF16)
        for first in range(0, 2 * half_rows, 256):
            rows = lowered_ref[first : first + 256, :]
            result = dot(rows, w_ref[...], NT) + bias_ref[...]
            qkv_ref[first : first + 256, :third] = (result[:, :third] * HEAD**-0.5).astype(BF16)
            qkv_ref[first : first + 256, third:] = result[:, third:].astype(BF16)

    return kernel_call(
        body,
        [shape(2 * half_rows, model), shape(2 * half_rows, width)],
        [at],
        [own, away, step_row, bias] + flat,
        [pltpu.VMEM((width, model), BF16)],
        4 * half_rows * model * width,
        "project_qkv",
    )


BLOCK_Q = 128
BLOCK_K = 256


def active_blocks(docs):
    length = docs.shape[0]
    q_docs, k_docs = docs.reshape(-1, BLOCK_Q), docs.reshape(-1, BLOCK_K)
    active = (k_docs[None, :, 0] <= q_docs[:, None, -1]) & (k_docs[None, :, -1] >= q_docs[:, None, 0])
    active = active.astype(jnp.int32)
    blocks = length // BLOCK_K
    order = jnp.arange(blocks)
    place = jnp.sum(active[:, None, :] * (order[None, :] < order[:, None])[None], axis=2)
    hit = active[:, :, None] * (place[:, :, None] == order[None, None, :])
    listed = jnp.sum(hit * order[None, :, None], axis=1)
    return jnp.concatenate([jnp.sum(active, axis=1), listed.reshape(-1)]).astype(jnp.int32)


def stacked(block):
    first = lax.broadcasted_iota(jnp.int32, block.shape, 1) < HEAD
    zero = jnp.zeros_like(block)
    return jnp.concatenate([jnp.where(first, block, zero), jnp.where(first, zero, block)])


def beside(pair):
    rows = pair.shape[0] // 2
    first = lax.broadcasted_iota(jnp.int32, (rows, LANES), 1) < HEAD
    return jnp.where(first, pair[:rows], pair[rows:])


def each_count(blocks_ref, at, query_blocks, key_blocks, do):
    count = blocks_ref[at]
    for number in range(1, key_blocks + 1):

        @pl.when(count == number)
        def _(number=number):
            do([blocks_ref[query_blocks + at * key_blocks + one] for one in range(number)])


def key_rows(block):
    return pl.ds(pl.multiple_of(block * BLOCK_K, BLOCK_K), BLOCK_K)


def attend(active, qkv, docs_column, docs_row, table_shape):
    length, width = qkv.shape
    pairs = width // (3 * LANES)
    key_blocks, query_blocks = length // BLOCK_K, length // BLOCK_Q
    fill = max(size for size in range(8, 1025, 8) if table_shape[0] % size == 0)
    fills = table_shape[0] // fill

    def body(
        active_ref, q_ref, k_ref, v_ref, column_ref, row_ref, o_ref, lse_ref, table_ref, zero_ref, sem
    ):
        def copy(index):
            return pltpu.make_async_copy(
                zero_ref, table_ref.at[pl.ds(index * fill, fill), :], sem.at[index]
            )

        @pl.when(pl.program_id(0) == 0)
        def _():
            zero_ref[...] = jnp.zeros_like(zero_ref)
            for index in range(fills):
                copy(index).start()

        @pl.loop(0, query_blocks)
        def _(at):
            here = pl.ds(pl.multiple_of(at * BLOCK_Q, BLOCK_Q), BLOCK_Q)

            def do(blocks):
                query = stacked(q_ref[here, :])
                column = column_ref[here, :]
                column = jnp.concatenate([column, column])
                scores = []
                peak = None
                for block in blocks:
                    raw = dot(query, k_ref[key_rows(block), :], NT)
                    scores.append(jnp.where(column == row_ref[block], raw, MASKED))
                    for lane in range(0, BLOCK_K, LANES):
                        part = scores[-1][:, lane : lane + LANES]
                        peak = part if peak is None else jnp.maximum(peak, part)
                peak = jnp.max(peak, axis=1, keepdims=True)
                sums, mixed = 0.0, 0.0
                for block, one in zip(blocks, scores):
                    weights = jnp.exp(one - peak)
                    for lane in range(0, BLOCK_K, LANES):
                        sums = sums + weights[:, lane : lane + LANES]
                    mixed = mixed + dot(weights.astype(BF16), v_ref[key_rows(block), :], NN)
                sums = jnp.sum(sums, axis=1, keepdims=True)
                o_ref[here, :] = beside(mixed / sums).astype(BF16)
                logs = jnp.broadcast_to(peak + jnp.log(sums), (2 * BLOCK_Q, LANES))
                lse_ref[here, :] = beside(logs)

            each_count(active_ref, at, query_blocks, key_blocks, do)

        @pl.when(pl.program_id(0) == pairs - 1)
        def _():
            for index in range(fills):
                copy(index).wait()

    def columns(kind):
        return pl.BlockSpec((length, LANES), lambda pair, *_: (0, kind * pairs + pair))

    grid_spec = pltpu.PrefetchScalarGridSpec(
        num_scalar_prefetch=1,
        grid=(pairs,),
        in_specs=[
            columns(0),
            columns(1),
            columns(2),
            pl.BlockSpec((length, 1), lambda pair, *_: (0, 0)),
            pl.BlockSpec(docs_row.shape, lambda pair, *_: (0, 0, 0)),
        ],
        out_specs=[columns(0), columns(0), pl.BlockSpec(memory_space=pl.ANY)],
        scratch_shapes=[
            pltpu.VMEM((fill, table_shape[1]), F32),
            pltpu.SemaphoreType.DMA((fills,)),
        ],
    )
    outs = [shape(length, pairs * LANES), shape(length, pairs * LANES, F32), shape(*table_shape, F32)]
    return pl.pallas_call(
        body,
        out_shape=outs,
        grid_spec=grid_spec,
        compiler_params=params(),
        cost_estimate=cost(10e9, [qkv, *outs]),
        name="attend",
    )(active, qkv, qkv, qkv, docs_column, docs_row)


def attend_back(active, qkv, grad_mixed, mixed, lse, docs_column, docs_row):
    length, width = qkv.shape
    pairs = width // (3 * LANES)
    key_blocks, query_blocks = length // BLOCK_K, length // BLOCK_Q

    def body(
        active_ref, q_ref, k_ref, v_ref, g_ref, o_ref, lse_ref, column_ref, row_ref,
        dq_ref, dk_ref, dv_ref, dk_sum, dv_sum,
    ):
        dk_sum[...] = jnp.zeros_like(dk_sum)
        dv_sum[...] = jnp.zeros_like(dv_sum)

        @pl.loop(0, query_blocks)
        def _(at):
            here = pl.ds(pl.multiple_of(at * BLOCK_Q, BLOCK_Q), BLOCK_Q)

            def do(blocks):
                query = stacked(q_ref[here, :])
                grad = stacked(g_ref[here, :])
                out = o_ref[here, :].astype(F32)
                out = jnp.concatenate([out, out])
                row_dot = jnp.sum(grad.astype(F32) * out, axis=1, keepdims=True)
                column = column_ref[here, :]
                column = jnp.concatenate([column, column])
                logs = lse_ref[here, :]
                logs = jnp.concatenate([logs[:, :1], logs[:, HEAD : HEAD + 1]])
                dq = 0.0
                for block in blocks:
                    rows = key_rows(block)
                    key, value = k_ref[rows, :], v_ref[rows, :]
                    raw = jnp.where(column == row_ref[block], dot(query, key, NT), MASKED)
                    weights = jnp.exp(raw - logs)
                    grad_weights = dot(grad, value, NT)
                    grad_scores = (weights * (grad_weights - row_dot)).astype(BF16)
                    dv_sum[rows, :] += dot(weights.astype(BF16), grad, TN)
                    dk_sum[rows, :] += dot(grad_scores, query, TN)
                    dq = dq + dot(grad_scores, key, NN)
                dq_ref[here, :] = (beside(dq) * HEAD**-0.5).astype(BF16)

            each_count(active_ref, at, query_blocks, key_blocks, do)

        dk_ref[...] = dk_sum[...].astype(BF16)
        dv_ref[...] = dv_sum[...].astype(BF16)

    def columns(kind):
        return pl.BlockSpec((length, LANES), lambda pair, *_: (0, kind * pairs + pair))

    grid_spec = pltpu.PrefetchScalarGridSpec(
        num_scalar_prefetch=1,
        grid=(pairs,),
        in_specs=[
            columns(0),
            columns(1),
            columns(2),
            columns(0),
            columns(0),
            columns(0),
            pl.BlockSpec((length, 1), lambda pair, *_: (0, 0)),
            pl.BlockSpec(docs_row.shape, lambda pair, *_: (0, 0, 0)),
        ],
        out_specs=[columns(0)] * 3,
        scratch_shapes=[pltpu.VMEM((length, LANES), F32)] * 2,
    )
    outs = [shape(length, pairs * LANES)] * 3
    return pl.pallas_call(
        body,
        out_shape=outs,
        grid_spec=grid_spec,
        compiler_params=params(),
        cost_estimate=cost(16e9, [qkv, grad_mixed, mixed, lse, *outs]),
        name="attend_back",
    )(active, qkv, qkv, qkv, grad_mixed, mixed, lse, docs_column, docs_row)


def join_weights(at, gathered, blocks, heights):
    halves, count, _, part = gathered.shape

    def body(at_ref, in_ref, *outs):
        first = 0
        for out, height in zip(outs, heights):
            for block in range(blocks):
                z = lax.rem(at_ref[0] - at_ref[2] * blocks - block + 2 * count, count)
                for half in range(halves):
                    x = lax.rem(at_ref[1] + half, halves)
                    out[block * height : (block + 1) * height, half * part : (half + 1) * part] = in_ref[
                        x, z, first : first + height, :
                    ]
            first += height

    return kernel_call(
        body,
        [shape(blocks * height, halves * part) for height in heights],
        [at],
        [gathered],
        (),
        0,
        "join_weights",
    )


def token_rows(ref, first, chunk, at, count, run):
    per = count // CHUNKS
    rows = []
    for rel in range(chunk * per, (chunk + 1) * per):
        natural = lax.rem(at - rel + count, count)
        rows.append(ref[pl.ds(pl.multiple_of(first + natural * run, run), run), :])
    return jnp.concatenate(rows)


def project_out(at, mixed, pieces, first, count):
    blocks, halves = len(pieces), len(pieces[0])
    part = pieces[0][0].shape[1]
    length, width = mixed.shape
    model = part * halves
    half_rows = length // 2
    rows = half_rows // CHUNKS
    flat = [one for row in pieces for one in row]

    def body(at_ref, mixed_ref, *refs):
        piece_refs, outs, w_ref = refs[: len(flat)], refs[len(flat) : -1], refs[-1]
        assemble(piece_refs, blocks, halves, part, first, width // blocks, 1, w_ref)
        for chunk in range(CHUNKS):
            for which in range(2):
                taken = token_rows(mixed_ref, which * half_rows, chunk, at_ref[0], count, half_rows // count)
                out = outs[chunk * 2 + which]
                out[...] = dot(taken, w_ref[...], NN).astype(out.dtype)

    return kernel_call(
        body,
        [shape(rows, model, F32), shape(rows, model)] * CHUNKS,
        [at],
        [mixed, *flat],
        [pltpu.VMEM((width, model), BF16)],
        2 * length * width * model,
        "project_out",
    )


def feed_forward(own, away, bias, up, down):
    rows, model = own.shape
    hidden = up.shape[0]
    step = 256

    def body(own_ref, away_ref, bias_ref, up_ref, down_ref, sum_ref, send_ref, act_ref, slope_ref, in_ref):
        in_ref[:rows, :] = own_ref[...]
        in_ref[rows:, :] = away_ref[...]
        for first in range(0, hidden, step):
            cut = slice(first, first + step)
            pre = dot(in_ref[...], up_ref[cut, :], NT) + bias_ref[:, cut]
            cdf = 0.5 * (1.0 + lax.erf(pre * (0.5**0.5)))
            act_ref[:, cut] = (pre * cdf).astype(BF16)
            density = jnp.exp(-0.5 * pre * pre) * (0.5 / jnp.pi) ** 0.5
            slope_ref[:, cut] = (cdf + pre * density).astype(BF16)
        send_ref[...] = dot(act_ref[rows:, :], down_ref[...], NN).astype(BF16)
        sum_ref[...] = dot(act_ref[:rows, :], down_ref[...], NN)

    return kernel_call(
        body,
        [shape(rows, model, F32), shape(rows, model), shape(2 * rows, hidden), shape(2 * rows, hidden)],
        [],
        [own, away, bias, up, down],
        [pltpu.VMEM((2 * rows, model), BF16)],
        8 * rows * model * hidden,
        "feed_forward",
    )


def feed_back(own, away, slope, up, down):
    rows, model = own.shape
    hidden = up.shape[0]
    step = 256

    def body(own_ref, away_ref, slope_ref, up_ref, down_ref, sum_ref, send_ref, pre_ref, total_ref, in_ref):
        in_ref[:rows, :] = own_ref[...]
        in_ref[rows:, :] = away_ref[...]
        for first in range(0, hidden, step):
            cut = slice(first, first + step)
            grad = dot(in_ref[...], down_ref[cut, :], NT) * slope_ref[:, cut].astype(F32)
            low = grad.astype(BF16)
            pre_ref[:, cut] = low
            total_ref[:, cut] = jnp.sum(low.astype(F32), axis=0, keepdims=True)
        send_ref[...] = dot(pre_ref[rows:, :], up_ref[...], NN).astype(BF16)
        sum_ref[...] = dot(pre_ref[:rows, :], up_ref[...], NN)

    return kernel_call(
        body,
        [shape(rows, model, F32), shape(rows, model), shape(2 * rows, hidden), shape(1, hidden, F32)],
        [],
        [own, away, slope, up, down],
        [pltpu.VMEM((2 * rows, model), BF16)],
        8 * rows * model * hidden,
        "feed_back",
    )


def weight_grad(lefts, rights, halves, name):
    rows, height = lefts[0].shape
    model = rights[0][0].shape[1]
    part = model // halves
    step = 256 if height % 256 == 0 else height
    flat = [one for chunk in rights for one in chunk]

    def body(*refs):
        left_refs = refs[: len(lefts)]
        right_refs = refs[len(lefts) : len(lefts) + len(flat)]
        outs = refs[len(lefts) + len(flat) : -1]
        all_ref = refs[-1]

        @pl.when(pl.program_id(0) == 0)
        def _():
            first = 0
            for ref in right_refs:
                all_ref[first : first + ref.shape[0], :] = ref[...]
                first += ref.shape[0]

        result = None
        for index, ref in enumerate(left_refs):
            term = dot(ref[...], all_ref[index * rows : (index + 1) * rows, :], TN)
            result = term if result is None else result + term
        for half, out in enumerate(outs):
            out[...] = result[:, half * part : (half + 1) * part].astype(BF16)

    return pl.pallas_call(
        body,
        out_shape=[shape(height, part)] * halves,
        grid=(height // step,),
        in_specs=[pl.BlockSpec((rows, step), lambda at: (0, at))] * len(lefts)
        + [pl.BlockSpec(one.shape, lambda at: (0, 0)) for one in flat],
        out_specs=[pl.BlockSpec((step, part), lambda at: (at, 0))] * halves,
        scratch_shapes=[pltpu.VMEM((rows * len(lefts), model), BF16)],
        compiler_params=params(),
        cost_estimate=cost(2 * rows * len(lefts) * height * model, [*lefts, *flat]),
        name=name,
    )(*lefts, *flat)


def mixed_grads(at, owns, aways, mixed, pieces, first, count):
    blocks, halves = len(pieces), len(pieces[0])
    length, width = mixed.shape
    part = pieces[0][0].shape[1]
    model = part * halves
    half_rows = length // 2
    per = half_rows // CHUNKS
    flat = [one for row in pieces for one in row]

    def body(at_ref, *refs):
        own_refs, away_refs = refs[:CHUNKS], refs[CHUNKS : 2 * CHUNKS]
        mixed_ref, refs = refs[2 * CHUNKS], refs[2 * CHUNKS + 1 :]
        piece_refs, grad_ref = refs[: len(flat)], refs[len(flat)]
        outs, (all_ref, w_ref) = refs[len(flat) + 1 : -2], refs[-2:]
        assemble(piece_refs, blocks, halves, part, first, width // blocks, 1, w_ref)
        run = half_rows // count
        for which, group in enumerate((own_refs, away_refs)):
            for rel in range(count):
                natural = lax.rem(at_ref[0] - rel + count, count)
                ref = group[rel * run // per]
                start = rel * run % per
                place = pl.multiple_of(which * half_rows + natural * run, run)
                all_ref[pl.ds(place, run), :] = ref[start : start + run, :]
        for start in range(0, length, 256):
            cut = slice(start, start + 256)
            grad_ref[cut, :] = dot(all_ref[cut, :], w_ref[...], NT).astype(BF16)
        result = dot(mixed_ref[...], all_ref[...], TN)
        for half, out in enumerate(outs):
            out[...] = result[:, half * part : (half + 1) * part].astype(BF16)

    return kernel_call(
        body,
        [shape(length, width)] + [shape(width, part)] * halves,
        [at],
        [*owns, *aways, mixed, *flat],
        [pltpu.VMEM((length, model), BF16), pltpu.VMEM((width, model), BF16)],
        4 * length * width * model,
        "mixed_grads",
    )


def return_rows(at, grads, pieces, count):
    length, third = grads[0].shape
    blocks, halves = len(pieces), len(pieces[0])
    part = pieces[0][0].shape[1]
    model = part * halves
    half_rows = length // 2
    flat = [one for row in pieces for one in row]

    def body(at_ref, q_ref, k_ref, v_ref, *rest):
        piece_refs, (sum_ref, send_ref, total_ref, w_ref) = rest[: len(flat)], rest[len(flat) :]
        assemble(piece_refs, blocks, halves, part, 0, third // blocks, 3, w_ref)
        run = half_rows // count
        per = half_rows // CHUNKS
        for which, out in ((1, send_ref), (0, sum_ref)):
            for chunk in range(CHUNKS):
                taken = jnp.concatenate(
                    [
                        token_rows(ref, which * half_rows, chunk, at_ref[0], count, run)
                        for ref in (q_ref, k_ref, v_ref)
                    ],
                    axis=1,
                )
                out[chunk * per : (chunk + 1) * per, :] = dot(taken, w_ref[...], NN).astype(out.dtype)
        for kind, ref in enumerate((q_ref, k_ref, v_ref)):
            total_ref[:, kind * third : (kind + 1) * third] = jnp.sum(
                ref[...].astype(F32), axis=0, keepdims=True
            )

    return kernel_call(
        body,
        [shape(half_rows, model, F32), shape(half_rows, model), shape(1, 3 * third, F32)],
        [at],
        [*grads, *flat],
        [pltpu.VMEM((3 * third, model), BF16)],
        6 * length * third * model,
        "return_rows",
    )


def qkv_grads(grads, lowered, halves):
    third = grads[0].shape[1]
    length, model = lowered.shape
    part = model // halves

    def body(q_ref, k_ref, v_ref, lowered_ref, *outs):
        for kind, ref in enumerate((q_ref, k_ref, v_ref)):
            result = dot(ref[...], lowered_ref[...], TN)
            for half, out in enumerate(outs):
                cut = slice(half * part, (half + 1) * part)
                out[kind * third : (kind + 1) * third, :] = result[:, cut].astype(BF16)

    return kernel_call(
        body,
        [shape(3 * third, part)] * halves,
        [],
        [*grads, lowered],
        (),
        6 * length * third * model,
        "qkv_grads",
    )


def place_rows(zeros, steps, tiles):
    count = steps.shape[0]

    def body(steps_ref, tiles_ref, zeros_ref, out_ref, sem):
        del zeros_ref
        copies = [
            pltpu.make_async_copy(
                tiles_ref.at[8 * one : 8 * one + 8, :],
                out_ref.at[pl.ds(pl.multiple_of(steps_ref[one] // 8 * 8, 8), 8), :],
                sem.at[one],
            )
            for one in range(count)
        ]
        for one in copies:
            one.start()
        for one in copies:
            one.wait()

    return pl.pallas_call(
        body,
        out_shape=jax.ShapeDtypeStruct(zeros.shape, zeros.dtype),
        in_specs=[
            pl.BlockSpec(memory_space=pltpu.SMEM),
            pl.BlockSpec(memory_space=pltpu.VMEM),
            pl.BlockSpec(memory_space=pl.ANY),
        ],
        out_specs=pl.BlockSpec(memory_space=pl.ANY),
        scratch_shapes=[pltpu.SemaphoreType.DMA((count,))],
        input_output_aliases={2: 0},
        name="place_rows",
    )(steps, tiles, zeros)


def swap(rows, axis):
    return lax.ppermute(rows, axis, [(0, 1), (1, 0)])


def pick(parts, index, at):
    return lax.dynamic_index_in_dim(parts, index, at, keepdims=False)


def join(*values):
    return lax.optimization_barrier(values)


def norm(rows):
    centered = rows - jnp.mean(rows, axis=-1, keepdims=True)
    inverse = lax.rsqrt(jnp.mean(centered * centered, axis=-1, keepdims=True) + NORM_EPS)
    return centered * inverse, inverse


def norm_back(normed, inverse, gain, grad):
    scaled = grad * gain
    mean_one = jnp.mean(scaled, axis=-1, keepdims=True)
    mean_two = jnp.mean(scaled * normed, axis=-1, keepdims=True)
    return (scaled - mean_one - normed * mean_two) * inverse


def total(values, axes):
    for axis in axes:
        size = lax.axis_size(axis)
        if size & (size - 1):
            values = lax.psum(values, axis)
            continue
        step = 1
        while step < size:
            values = values + lax.ppermute(values, axis, [(one, one ^ step) for one in range(size)])
            step *= 2
    return values


def shards(
    inputs,
    timesteps,
    segments,
    table,
    w_qkv,
    qv_bias,
    w_out,
    w_up,
    ffn_bias,
    w_down,
    out_biases,
    norm_gains,
    norm_biases,
    cotangent,
):
    fsdp_size, ctx_size = lax.axis_size("fsdp"), lax.axis_size("ctx")
    tz_size, ty_size = lax.axis_size("tz"), lax.axis_size("ty")
    fsdp_at, ctx_at = lax.axis_index("fsdp"), lax.axis_index("ctx")
    tz_at, ty_at = lax.axis_index("tz"), lax.axis_index("ty")
    seq_here, piece, model = inputs.shape
    length = segments.shape[1]
    part = model // fsdp_size
    half_rows = length // ctx_size
    chunk_rows = half_rows // CHUNKS
    run = ty_size * piece
    block_heads = w_qkv.shape[2] // HEAD
    cut = block_heads % ctx_size == 0
    blocks = tz_size if cut else tz_size // ctx_size

    def shift(core, block):
        return block if cut else core * blocks + block

    def ring(block, sign):
        return [
            (core * tz_size + z, core * tz_size + (z + sign * shift(core, block)) % tz_size)
            for core in range(ctx_size)
            for z in range(tz_size)
        ]

    def along(values, block, sign):
        if cut and block == 0:
            return values
        return lax.ppermute(values, ("ctx", "tz"), ring(block, sign))

    def halves_order(values):
        if fsdp_size != 2:
            return values
        turned = jnp.concatenate([values[..., part:], values[..., :part]], axis=-1)
        return jnp.where(fsdp_at == 0, values, turned)

    def across(values):
        if fsdp_size == 2:
            return [values, swap(values, "fsdp")]
        gathered = lax.all_gather(values, "fsdp", axis=0, tiled=False)
        return [gathered[one] for one in range(fsdp_size)]

    def share(values):
        if not cut:
            return values
        return pick(values.reshape((ctx_size, -1) + values.shape[1:]), ctx_at, 0)

    turned = jnp.transpose(w_qkv, (0, 2, 1))
    if cut:
        turned = pick(turned.reshape(3, ctx_size, -1, part), ctx_at, 1)
    qkv_rows = turned.reshape(-1, part)
    third = qkv_rows.shape[0] // 3
    qv_share = pick(qv_bias.reshape(2, ctx_size, -1), ctx_at, 1) if cut else qv_bias
    ffn_share = share(ffn_bias)
    bias_flat = jnp.concatenate([qv_share.reshape(-1), ffn_share])
    bias_rows = -(-bias_flat.shape[0] // (16 * part)) * 16
    bias_block = jnp.pad(bias_flat, (0, bias_rows * part - bias_flat.shape[0])).reshape(-1, part)
    out_rows = share(w_out)
    first_block = jnp.concatenate([qkv_rows, out_rows, bias_block])
    rest_block = jnp.concatenate([share(w_up.T), share(w_down)])
    out_height = out_rows.shape[0]
    hidden_height = ffn_share.shape[0]
    rest_all = lax.all_gather(rest_block, ("fsdp", "tz"), axis=0, tiled=True)
    rest_all = rest_all.reshape(fsdp_size, tz_size, 2 * hidden_height, part)

    first_pieces = [across(along(first_block, block, 1)) for block in range(blocks)]

    def arrive(values):
        got = [pick(values, tz_at, 0)]
        for step in range(1, tz_size):
            sent = pick(values, (tz_at + step) % tz_size, 0)
            got.append(lax.ppermute(sent, "tz", [(z, (z + step) % tz_size) for z in range(tz_size)]))
        return jnp.stack(got)

    def depart(values):
        values = values.reshape(tz_size, piece, model)
        result = jnp.zeros_like(values)
        for step in range(tz_size):
            got = values[step]
            if step:
                got = lax.ppermute(got, "tz", [(z, (z - step) % tz_size) for z in range(tz_size)])
            result = lax.dynamic_update_index_in_dim(result, got, (tz_at + step) % tz_size, 0)
        return result

    def over_y(values):
        if ty_size != 2:
            return lax.all_gather(values, "ty", axis=1, tiled=False)
        own = (jnp.arange(2) == ty_at).reshape(1, 2, 1, 1)
        return jnp.where(own, values[:, None], swap(values, "ty")[:, None])

    def half_of(values):
        return over_y(arrive(halves_order(values))).reshape(half_rows, model)

    own_inputs = half_of(inputs)
    away_inputs = swap(own_inputs, "ctx")
    own_grad = half_of(join(cotangent, own_inputs)[0])

    biases = [row[0][3 * third + out_height :].reshape(-1)[: bias_flat.shape[0]].astype(F32) for row in first_pieces]
    q_bias = jnp.concatenate([one[:third] for one in biases])
    v_bias = jnp.concatenate([one[third : 2 * third] for one in biases])
    qkv_bias = jnp.concatenate([q_bias, jnp.zeros_like(q_bias), v_bias])[None]
    hidden_bias = jnp.concatenate([one[2 * third :] for one in biases])[None]
    biases_out = halves_order(out_biases.astype(F32))
    gains = halves_order(norm_gains.astype(F32))
    offsets = halves_order(norm_biases.astype(F32))

    sequence = fsdp_at * seq_here + tz_at
    docs = pick(segments, tz_at, 0).reshape(ctx_size, half_rows)
    docs = jnp.concatenate([pick(docs, ctx_at, 0), pick(docs, 1 - ctx_at, 0)])
    docs_column, docs_row = docs[:, None], docs.reshape(-1, 1, BLOCK_K)
    active = active_blocks(docs)
    step_row = halves_order(lax.dynamic_slice_in_dim(table, timesteps[sequence], 1, 0).astype(F32))
    x_first = fsdp_at if fsdp_size == 2 else 0
    at = jnp.stack([tz_at, x_first, 0 if cut else ctx_at]).astype(jnp.int32)

    lowered, qkv = project_qkv(at, own_inputs, away_inputs, step_row, qkv_bias, first_pieces, tz_size)
    mixed, lse, zero_table = attend(active, qkv, docs_column, docs_row, (table.shape[0], part))
    up_all, down_all = join_weights(at, rest_all, blocks, [hidden_height, hidden_height])
    start = own_inputs.astype(F32) + step_row

    def reduce_rows(own, send):
        summed = (own + swap(send, "ctx").astype(F32)).astype(BF16)
        if ty_size != 2:
            return lax.psum(summed.astype(F32), "ty")
        return summed.astype(F32) + swap(summed, "ty").astype(F32)

    def rows_of(values, chunk):
        return values[chunk * chunk_rows : (chunk + 1) * chunk_rows]

    partials = project_out(at, mixed, first_pieces, 3 * third, tz_size)
    every = range(CHUNKS)
    normed_one, inverse_one, hidden, hidden_own, hidden_away = [], [], [], [], []
    for chunk in every:
        attended = reduce_rows(partials[2 * chunk], partials[2 * chunk + 1]) + biases_out[0]
        normed, inverse = norm(rows_of(start, chunk) + attended)
        normed_one.append(normed)
        inverse_one.append(inverse)
        hidden.append(normed * gains[0] + offsets[0])
        hidden_own.append(hidden[-1].astype(BF16))
        hidden_away.append(swap(hidden_own[-1], "ctx"))
    forward = [
        feed_forward(hidden_own[chunk], hidden_away[chunk], hidden_bias, up_all, down_all)
        for chunk in every
    ]
    outputs, normed_two, grad_final, grad_second, ffn_own, ffn_away = [], [], [], [], [], []
    for chunk in every:
        ffn_out = reduce_rows(forward[chunk][0], forward[chunk][1]) + biases_out[1]
        normed, inverse = norm(hidden[chunk] + ffn_out)
        normed_two.append(normed)
        outputs.append((normed * gains[1] + offsets[1]).astype(BF16))
        grad_final.append(rows_of(own_grad, chunk).astype(F32))
        grad_second.append(norm_back(normed, inverse, gains[1], grad_final[-1]))
        ffn_own.append(grad_second[-1].astype(BF16))
        ffn_away.append(swap(ffn_own[-1], "ctx"))
    activated = [one[2] for one in forward]
    backward = [
        feed_back(ffn_own[chunk], ffn_away[chunk], forward[chunk][3], up_all, down_all)
        for chunk in every
    ]
    grad_pre = [one[2] for one in backward]
    grad_down = weight_grad(activated, list(zip(ffn_own, ffn_away)), fsdp_size, "down_grad")
    grad_up = weight_grad(grad_pre, list(zip(hidden_own, hidden_away)), fsdp_size, "up_grad")
    grad_hidden, grad_first, first_own, first_away = [], [], [], []
    for chunk in every:
        grad_hidden.append(grad_second[chunk] + reduce_rows(backward[chunk][0], backward[chunk][1]))
        grad_first.append(norm_back(normed_one[chunk], inverse_one[chunk], gains[0], grad_hidden[-1]))
        first_own.append(grad_first[-1].astype(BF16))
        first_away.append(swap(first_own[-1], "ctx"))
    grad_mixed, *grad_out = mixed_grads(at, first_own, first_away, mixed, first_pieces, 3 * third, tz_size)
    grads = attend_back(active, qkv, grad_mixed, mixed, lse, docs_column, docs_row)
    start_own, start_send, head_sums = return_rows(at, grads, first_pieces, tz_size)
    grad_qkv = qkv_grads(grads, lowered, fsdp_size)

    def own_y(values):
        return pick(values.reshape(tz_size, ty_size, piece, model), ty_at, 1)

    output = halves_order(depart(own_y(jnp.concatenate(outputs))))

    summed = start_own + swap(start_send, "ctx").astype(F32)
    if ty_size == 2:
        grid = summed.reshape(tz_size, 2, piece, model)
        returned = pick(grid, ty_at, 1) + swap(pick(grid, 1 - ty_at, 1).astype(BF16), "ty").astype(F32)
    else:
        grid = summed.astype(BF16).reshape(tz_size, ty_size, piece, model)
        returned = lax.psum_scatter(grid, "ty", scatter_dimension=1, tiled=False).astype(F32)
    grad_start = own_y(jnp.concatenate(grad_first)) + returned
    grad_inputs = halves_order(depart(grad_start.astype(BF16)))

    def over_x(grads):
        if fsdp_size == 2:
            return (grads[0].astype(F32) + swap(grads[1], "fsdp").astype(F32)).astype(BF16)
        return lax.psum_scatter(jnp.stack(grads), "fsdp", scatter_dimension=0, tiled=False)

    def release(*parts):
        summed, kinds = [], [one[1] for one in parts]
        for grads, number in parts:
            one = over_x(grads).reshape(number, blocks, -1, part)
            summed.append(one)
        heights = [one.shape[0] * one.shape[2] for one in summed]
        own = None
        for block in range(blocks):
            sent = jnp.concatenate([one[:, block].reshape(-1, part) for one in summed])
            got = along(sent, block, -1).astype(F32)
            own = got if own is None else own + got
        pieces = own.reshape(-1, ctx_size, part // ctx_size)
        kept = pick(pieces, ctx_at, 1)
        away = swap(pick(pieces, 1 - ctx_at, 1).astype(BF16), "ctx").astype(F32)
        results, first = [], 0
        for height, number in zip(heights, kinds):
            one, other = kept[first : first + height], away[first : first + height]
            first += height
            if not cut:
                results.append((one + other).reshape(number, -1, one.shape[-1]))
                continue
            one, other = (value.reshape(number, 1, -1, value.shape[-1]) for value in (one, other))
            order = (jnp.arange(2) == ctx_at)[None, :, None, None]
            results.append(jnp.where(order, one, other).reshape(number, -1, one.shape[-1]))
        return results

    red_down, red_up = release((grad_down, 1), (grad_up, 1))
    red_down, red_up = red_down[0], red_up[0].T
    red_out, red_qkv = release((grad_out, 1), (grad_qkv, 3))
    red_out, red_qkv = red_out[0], jnp.transpose(red_qkv, (0, 2, 1))

    def spread(values):
        kinds, _, width = values.shape
        if cut:
            full = jnp.zeros((kinds, tz_size, ty_size, ctx_size, width), F32)
        else:
            full = jnp.zeros((kinds, tz_size, ty_size, 1, width), F32)
        core = ctx_at if cut else 0
        for block in range(blocks):
            away = block if cut else ctx_at * blocks + block
            full = lax.dynamic_update_slice(
                full,
                values[:, block].reshape(kinds, 1, 1, 1, width),
                (0, (tz_at - away) % tz_size, ty_at, core, 0),
            )
        return full.reshape(kinds, -1)

    def rows_sum(values):
        return sum(jnp.sum(one.astype(F32), axis=0) for one in values)

    once = (ty_at == 0).astype(F32)
    row_sums = once * halves_order(
        jnp.stack(
            [
                rows_sum([a * b for a, b in zip(grad_hidden, normed_one)]),
                rows_sum([a * b for a, b in zip(grad_final, normed_two)]),
                rows_sum(grad_hidden),
                rows_sum(grad_final),
                rows_sum(first_own),
                rows_sum(ffn_own),
                rows_sum(grad_first),
            ]
        )
    )
    heads = head_sums.reshape(3, blocks, -1)
    first_cut = lax.reduce_precision(head_sums, 8, 7)
    second_cut = lax.reduce_precision(head_sums - first_cut, 8, 7)
    third_cut = head_sums - first_cut - second_cut
    split = jnp.concatenate([first_cut, second_cut, third_cut]).astype(BF16)
    seq_sum = 0.0
    for block in range(blocks):
        own_columns = split.reshape(3, 3, blocks, -1)[:, :, block].reshape(3, -1)
        seq_sum = seq_sum + jnp.concatenate(
            [
                jnp.sum(dot(own_columns, one[: 3 * third], NN), axis=0)
                for one in first_pieces[block]
            ]
        )
    seq_sum = halves_order(seq_sum) + row_sums[6]
    slots = jnp.zeros((timesteps.shape[0], model), F32)
    slots = lax.dynamic_update_index_in_dim(slots, seq_sum, sequence, 0)
    sums = total(
        jnp.concatenate(
            [
                row_sums[:6],
                spread(heads[::2]),
                spread(sum(one[3] for one in backward).reshape(1, blocks, -1)).reshape(-1, model),
                slots,
            ]
        ),
        ("ctx", "ty", "fsdp", "tz"),
    )
    hidden_rows = tz_size * ty_size * hidden_height * (ctx_size if cut else 1) // model
    seq_sums = lax.dynamic_slice_in_dim(sums[8 + hidden_rows :], fsdp_at * part, part, 1)
    tile_rows = (timesteps // 8 * 8)[:, None] + jnp.arange(8)[None]
    match = (tile_rows[:, :, None] == timesteps[None, None, :]).astype(F32)
    tiles = jnp.sum(match[..., None] * seq_sums[None, None], axis=2).reshape(-1, part)
    grad_table = place_rows(zero_table, timesteps, tiles)
    return (
        output,
        grad_inputs,
        grad_table,
        red_qkv,
        sums[6:8],
        red_out,
        red_up,
        sums[8 : 8 + hidden_rows].reshape(-1),
        red_down,
        sums[4:6],
        sums[:2],
        sums[2:4],
    )


def solution(mesh):
    rows = P("fsdp", ("ctx", "tz", "ty"), None)
    tp = ("tz", "ty")
    in_specs = (
        rows,
        P(),
        P("fsdp", None),
        P(),
        P(None, "fsdp", tp),
        P(None, tp),
        P(tp, "fsdp"),
        P("fsdp", tp),
        P(tp),
        P(tp, "fsdp"),
        P(),
        P(),
        P(),
        rows,
    )
    out_specs = (
        rows,
        rows,
        P(None, "fsdp"),
        P(None, ("fsdp", "ctx"), tp),
        P(),
        P(tp, ("fsdp", "ctx")),
        P(("fsdp", "ctx"), tp),
        P(),
        P(tp, ("fsdp", "ctx")),
        P(),
        P(),
        P(),
    )

    def step(inputs, *rest):
        fsdp, ctx, tp_size = (mesh.shape[axis] for axis in ("fsdp", "ctx", "tp"))
        tz_size = inputs.shape[0] // fsdp
        devices = mesh.devices.reshape(fsdp, ctx, tz_size, tp_size // tz_size)
        split = Mesh(devices, ("fsdp", "ctx", "tz", "ty"))
        return jax.shard_map(
            shards, mesh=split, in_specs=in_specs, out_specs=out_specs, check_vma=False
        )(inputs, *rest)

    return step
```
